256 devices in a mesh: dp: 8 (over x, core), vocab: 32 (over y, z).
Axes of the slice: x: 4, y: 4, z: 8, core: 2. Of those that a mesh axis runs over, the one named last changes fastest.
Arguments:
- head_input: bfloat16 [1024, 8192], P(('dp', 'vocab')), may hold values from -250 to 250
- body_input: bfloat16 [1024, 8192], P(('dp', 'vocab')), may hold values from -6 to 6
- head_weight: bfloat16 [16384, 8192], P('vocab'), may hold values from -0.0625 to 0.0625
- gate_weight: bfloat16 [8192, 14336], P('dp', 'vocab'), may hold values from -0.0625 to 0.0625
- up_weight: bfloat16 [8192, 14336], P('dp', 'vocab'), may hold values from -0.0625 to 0.0625
- down_weight: bfloat16 [8192, 14336], P('dp', 'vocab'), may hold values from -0.046875 to 0.046875
- tile_ids: int32 [2048, 128], P(('dp', 'vocab')), may hold values from 0 to 16383, as said below
- tile_probs: bfloat16 [2048, 128], P(('dp', 'vocab')), may hold values from 0 to 1, as said below
- tile_slot: int32 [1024], P('dp'), may hold values from 0 to 255, as said below
Outputs:
- input_grad: bfloat16 [1024, 8192], P('dp', 'vocab')
The draws below stay inside these ranges and needn't reach their ends.
Inputs may be any that keep to these rules, and one draw needn't show every extreme that they name: `tile_ids`: each stored slot lists 128 distinct token ids. `tile_probs`: in every slot the probabilities are positive and sum to at most 0.95. `tile_slot`: A group's store of 256 slots lies on the devices of one index of dp in order of vocab, 8 slots a device; rows of a group use distinct slots, so half of the slots hold no row's tile and are never read; in every group all 8 slots of some device are used, and which device varies.
All inputs are finite; a program needn't handle non-finite values.
Results may differ from the reference program's by a relative error of at most 0.02.
Values may be sent and summed in bfloat16 or wider, within the bound.
No kernel may reach another device: no remote copies, remote signals or barrier semaphores. Data moves between devices by JAX's collectives and lax.ppermute only.
A program may use at most 128 MiB of HBM per device.

```python
import jax
import jax.numpy as jnp
from jax import lax

D = 8192
FF = 14336
VOCAB = 16384
K = 128
MICRO = 2
MB_ROWS = 64
LOSS_SCALE = 1024
ROWS = 1024
STORE = 256
SLOTS = 8
VOCAB_DEV = 512
FF_DEV = 448
N_VOCAB = 32


def draw_head_input(key, part):
    first = jax.random.fold_in(key, 0)
    values = jnp.clip(jax.random.normal(first, (ROWS, D), jnp.float32), -6.0, 6.0)
    values = values * 3.0
    return values.astype(jnp.bfloat16)


def draw_tile_ids(key, part):
    count = 2 * ROWS
    first, second = jax.random.split(key)
    popular = jax.random.randint(first, (VOCAB,), 0, 4) * 4096
    noise = jax.random.randint(second, (count, VOCAB), 0, 4096)
    scores = (noise + popular[None, :]) * VOCAB + jnp.arange(VOCAB, dtype=jnp.int32)[None, :]
    return lax.top_k(scores, K)[1].astype(jnp.int32)


def draw_tile_probs(key, part):
    count = 2 * ROWS
    first, second = jax.random.split(key)
    levels = jax.random.uniform(first, (count, K), jnp.float32, 0.1, 1.0)
    factor = jax.random.uniform(second, (count, 1), jnp.float32, 0.2, 1.0)
    return (0.95 / K * levels * factor).astype(jnp.bfloat16)


def draw_tile_slot(key, part):
    group_rows = MICRO * MB_ROWS
    groups = ROWS // group_rows

    def one_group(index):
        group_key = jax.random.fold_in(key, index)
        busy_key, score_key, perm_key = jax.random.split(group_key, 3)
        busy = jax.random.randint(busy_key, (), 0, STORE // SLOTS)
        places = jnp.arange(STORE, dtype=jnp.int32)
        forced = (places // SLOTS == busy) | (places == 0) | (places == STORE - 1)
        scores = jax.random.randint(score_key, (STORE,), 0, 1 << 20) + jnp.where(forced, 0, 1 << 20)
        order = jnp.argsort(scores * STORE + places, stable=True).astype(jnp.int32)
        shuffle = jax.random.permutation(perm_key, group_rows)
        return jnp.zeros((group_rows,), jnp.int32).at[shuffle].set(order[:group_rows])
    return jax.vmap(one_group)(jnp.arange(groups, dtype=jnp.int32)).reshape(ROWS)


def steps_of(rng, extent, cuts, least, high):
    def one(dim, shards_of):
        steps = jax.random.uniform(jax.random.fold_in(jax.random.fold_in(rng, 6), dim), (shards_of,), jnp.float32, least / len(cuts), high / len(cuts))
        return jnp.repeat(jnp.exp(steps), extent[dim] // shards_of).reshape((-1,) + (1,) * (len(extent) - dim - 1))

    loudness = one(*cuts[0])
    for cut in cuts[1:]:
        loudness = loudness * one(*cut)
    return loudness


def bell_draw(rng, extent, width, most, pieces=(), kind=jnp.bfloat16):
    values = width * jax.random.normal(rng, extent, jnp.float32)
    if pieces:
        values = values * steps_of(rng, extent, pieces, -0.22, 0.18)
    return jnp.clip(values, -most, most).astype(kind)


def setup_inputs(seed: int = 0) -> dict:
    splits = jax.random.split(jax.random.key(seed), 10)
    return {
        "head_input": draw_head_input(jax.random.fold_in(splits[9], 71), 0),
        "body_input": bell_draw(splits[1], (ROWS, D), 1.0, 6.0, ((0, 256),)),
        "head_weight": bell_draw(splits[2], (VOCAB, D), D ** -0.5, 0.0625, ((0, 32),)),
        "gate_weight": bell_draw(splits[3], (D, FF), D ** -0.5, 0.0625, ((0, 8), (1, 32))),
        "up_weight": bell_draw(splits[4], (D, FF), D ** -0.5, 0.0625, ((0, 8), (1, 32))),
        "down_weight": bell_draw(splits[5], (D, FF), FF ** -0.5, 0.046875, ((0, 8), (1, 32))),
        "tile_ids": draw_tile_ids(jax.random.fold_in(splits[9], 71), 0),
        "tile_probs": draw_tile_probs(jax.random.fold_in(splits[9], 71), 0),
        "tile_slot": draw_tile_slot(jax.random.fold_in(splits[9], 71), 0),
    }


def group_grad(head_rows, body_rows, slots, store_ids, store_probs, head_weight, gate_weight, up_weight, down_weight):
    count = head_rows.shape[0]
    row_ids = store_ids[slots]
    row_probs = store_probs[slots].astype(jnp.float32)
    lines = jnp.broadcast_to(jnp.arange(count, dtype=jnp.int32)[:, None], row_ids.shape)
    teacher = jnp.zeros((count, VOCAB), jnp.float32).at[lines, row_ids].add(row_probs)
    picked = jnp.zeros((count, VOCAB), jnp.bool_).at[lines, row_ids].set(True)
    tail_mass = 1.0 - lax.optimization_barrier(jnp.sum(row_probs, axis=1, keepdims=True))
    logits = jnp.dot(head_rows, head_weight.T, preferred_element_type=jnp.float32)
    row_max = lax.optimization_barrier(jnp.max(logits, axis=1, keepdims=True))
    rest = jnp.where(picked, -1e+30, logits)
    rest_max = lax.optimization_barrier(jnp.max(rest, axis=1, keepdims=True))
    top_sum = lax.optimization_barrier(jnp.sum(jnp.where(picked, jnp.exp(logits - row_max), 0.0), axis=1, keepdims=True))
    rest_exp = jnp.where(picked, 0.0, jnp.exp(rest - rest_max))
    rest_sum = lax.optimization_barrier(jnp.sum(rest_exp, axis=1, keepdims=True))
    total = top_sum + rest_sum * jnp.exp(rest_max - row_max)
    student = jnp.exp(logits - row_max) / total
    spread = rest_exp / rest_sum
    top_share = top_sum / total
    logit_grad = (LOSS_SCALE * (student * (1.0 - tail_mass) + jnp.where(picked, tail_mass * student - teacher, -tail_mass * top_share * spread))).astype(jnp.bfloat16)

    def head_block(carry, index):
        grad_block = lax.dynamic_slice_in_dim(logit_grad, index * VOCAB_DEV, VOCAB_DEV, 1)
        weight_block = lax.dynamic_slice_in_dim(head_weight, index * VOCAB_DEV, VOCAB_DEV, 0)
        part = jnp.dot(grad_block, weight_block, preferred_element_type=jnp.float32).astype(jnp.bfloat16)
        part = lax.optimization_barrier(part)
        return (carry + part.astype(jnp.float32), None)
    head_sum, _ = lax.scan(head_block, jnp.zeros((count, D), jnp.float32), jnp.arange(N_VOCAB, dtype=jnp.int32))
    head_grad = head_sum.astype(jnp.bfloat16)
    gate_act = jnp.dot(body_rows, gate_weight, preferred_element_type=jnp.float32)
    up_act = jnp.dot(body_rows, up_weight, preferred_element_type=jnp.float32)
    down_grad = jnp.dot(head_grad, down_weight, preferred_element_type=jnp.float32)
    sigma = jax.nn.sigmoid(gate_act)
    gate_grad = (down_grad * up_act * sigma * (1.0 + gate_act * (1.0 - sigma))).astype(jnp.bfloat16)
    up_grad = (down_grad * gate_act * sigma).astype(jnp.bfloat16)

    def body_block(carry, index):
        gate_part = lax.dynamic_slice_in_dim(gate_grad, index * FF_DEV, FF_DEV, 1)
        up_part = lax.dynamic_slice_in_dim(up_grad, index * FF_DEV, FF_DEV, 1)
        gate_cols = lax.dynamic_slice_in_dim(gate_weight, index * FF_DEV, FF_DEV, 1)
        up_cols = lax.dynamic_slice_in_dim(up_weight, index * FF_DEV, FF_DEV, 1)
        part = jnp.dot(gate_part, gate_cols.T, preferred_element_type=jnp.float32) + jnp.dot(up_part, up_cols.T, preferred_element_type=jnp.float32)
        part = lax.optimization_barrier(part.astype(jnp.bfloat16))
        return (carry + part.astype(jnp.float32), None)
    branch, _ = lax.scan(body_block, jnp.zeros((count, D), jnp.float32), jnp.arange(N_VOCAB, dtype=jnp.int32))
    return (head_grad.astype(jnp.float32) + branch).astype(jnp.bfloat16)

def reference(head_input, body_input, head_weight, gate_weight, up_weight, down_weight, tile_ids, tile_probs, tile_slot):
    group_rows = MICRO * MB_ROWS
    groups = head_input.shape[0] // group_rows

    def one_group(index):
        head_rows = lax.dynamic_slice_in_dim(head_input, index * group_rows, group_rows, 0)
        body_rows = lax.dynamic_slice_in_dim(body_input, index * group_rows, group_rows, 0)
        slots = lax.dynamic_slice_in_dim(tile_slot, index * group_rows, group_rows, 0)
        store_ids = lax.dynamic_slice_in_dim(tile_ids, index * STORE, STORE, 0)
        store_probs = lax.dynamic_slice_in_dim(tile_probs, index * STORE, STORE, 0)
        return group_grad(head_rows, body_rows, slots, store_ids, store_probs, head_weight, gate_weight, up_weight, down_weight)
    result = lax.map(one_group, jnp.arange(groups, dtype=jnp.int32))
    return result.reshape(head_input.shape[0], D)
```

```python
import jax
import jax.numpy as jnp
from jax import lax
from jax.experimental import pallas as pl
from jax.sharding import PartitionSpec as P


LOSS_SCALE = 1024
NX, NY, NZ, CORES = 4, 4, 8, 2
RADIX = 128

Y_GROUPS = [[y * NZ + z for y in range(NY)] for z in range(NZ)]
Z_GROUPS = [[y * NZ + z for z in range(NZ)] for y in range(NY)]
SWAP_XY = [
    (
        (x * CORES + c) * NY * NZ + y * NZ + z,
        (y * CORES + c) * NY * NZ + x * NZ + z,
    )
    for x in range(NX)
    for c in range(CORES)
    for y in range(NY)
    for z in range(NZ)
]
NT = (((1,), (1,)), ((), ()))


def exchange(blocks, groups=None):
    return lax.all_to_all(blocks, "vocab", 0, 0, axis_index_groups=groups)


def replicate(block, copies):
    return jnp.broadcast_to(block[None], (copies,) + block.shape)


def as_tiles(rows):
    count, width = rows.shape
    return rows.reshape(count, width // 128, 128).transpose(1, 0, 2).reshape(-1, 128)


def from_tiles(blocks, rows):
    shards, size, lanes = blocks.shape
    blocks = blocks.reshape(shards, size // rows, rows, lanes).transpose(0, 2, 1, 3)
    return blocks.reshape(shards * rows, size // rows * lanes)


def add_blocks(blocks):
    return jnp.sum(blocks.astype(jnp.float32), axis=0)


def wide_kernel(rows_ref, weight_ref, out_ref):
    half = weight_ref.shape[2]
    total = lax.dot_general(
        rows_ref[:, :half], weight_ref[0], NT, preferred_element_type=jnp.float32
    )
    total += lax.dot_general(
        rows_ref[:, half:], weight_ref[1], NT, preferred_element_type=jnp.float32
    )
    out_ref[0] = total.astype(out_ref.dtype)


def wide(rows, weight):
    count = rows.shape[0]
    blocks, hidden, half = weight.shape
    parts = blocks // CORES
    return pl.pallas_call(
        wide_kernel,
        grid=(parts,),
        in_specs=[
            pl.BlockSpec(rows.shape, lambda i: (0, 0)),
            pl.BlockSpec((CORES, hidden, half), lambda i: (i, 0, 0)),
        ],
        out_specs=pl.BlockSpec((1, count, hidden), lambda i: (i, 0, 0)),
        out_shape=jax.ShapeDtypeStruct((parts, count, hidden), jnp.bfloat16),
        cost_estimate=pl.CostEstimate(
            flops=2 * count * blocks * hidden * half,
            bytes_accessed=2 * (weight.size + rows.size),
            transcendentals=0,
        ),
        name="wide",
    )(rows, weight)


def branch_kernel(gate_ref, up_ref, gate_weight_ref, up_weight_ref, out_ref):
    total = None
    for i in range(gate_ref.shape[0]):
        for act, weight in ((gate_ref, gate_weight_ref), (up_ref, up_weight_ref)):
            part = jnp.dot(act[i], weight[i, 0], preferred_element_type=jnp.float32)
            total = part if total is None else total + part
    out_ref[0] = total.astype(out_ref.dtype)


def branch_blocks(gate, up, gate_weight, up_weight):
    parts, count, hidden = gate.shape
    half = gate_weight.shape[2]
    share = CORES * half // NZ
    per = half // share
    gate_weight = gate_weight.reshape(parts, CORES, hidden, half)
    up_weight = up_weight.reshape(parts, CORES, hidden, half)
    weight_spec = pl.BlockSpec((parts, 1, hidden, share), lambda i: (0, i // per, 0, i % per))
    act_spec = pl.BlockSpec(gate.shape, lambda i: (0, 0, 0))
    return pl.pallas_call(
        branch_kernel,
        grid=(NZ,),
        in_specs=[act_spec, act_spec, weight_spec, weight_spec],
        out_specs=pl.BlockSpec((1, count, share), lambda i: (i, 0, 0)),
        out_shape=jax.ShapeDtypeStruct((NZ, count, share), jnp.bfloat16),
        cost_estimate=pl.CostEstimate(
            flops=4 * count * gate_weight.size,
            bytes_accessed=4 * gate_weight.size,
            transcendentals=0,
        ),
        name="branch",
    )(gate, up, gate_weight, up_weight)


def head_kernel(grad_ref, weight_ref, out_ref):
    for i in range(out_ref.shape[0]):
        share = out_ref.shape[2]
        out_ref[i] = jnp.dot(
            grad_ref[...],
            weight_ref[:, i * share : (i + 1) * share],
            preferred_element_type=jnp.float32,
        ).astype(out_ref.dtype)


def head_blocks(grad, weight):
    count, vocab = grad.shape
    width = weight.shape[1]
    parts = NY * NZ
    share = width // parts
    step = 4
    return pl.pallas_call(
        head_kernel,
        grid=(parts // step,),
        in_specs=[
            pl.BlockSpec(grad.shape, lambda i: (0, 0)),
            pl.BlockSpec((vocab, step * share), lambda i: (0, i)),
        ],
        out_specs=pl.BlockSpec((step, count, share), lambda i: (i, 0, 0)),
        out_shape=jax.ShapeDtypeStruct((parts, count, share), jnp.bfloat16),
        cost_estimate=pl.CostEstimate(
            flops=2 * count * weight.size,
            bytes_accessed=2 * weight.size,
            transcendentals=0,
        ),
        name="head",
    )(grad, weight)


def marks_kernel(columns_ref, probs_ref, out_ref):
    _, entries = columns_ref.shape
    lanes = lax.broadcasted_iota(jnp.int32, out_ref.shape, 1)
    columns = columns_ref[...]
    probs = probs_ref[...]
    marks = jnp.full(out_ref.shape, -1.0, jnp.float32)
    for k in range(entries):
        marks = jnp.where(lanes == columns[:, k : k + 1], probs[:, k : k + 1], marks)
    out_ref[...] = marks


def make_marks(columns, probs, vocab):
    count, entries = columns.shape
    step = 16
    spec = pl.BlockSpec((step, entries), lambda i: (i, 0))
    return pl.pallas_call(
        marks_kernel,
        grid=(count // step,),
        in_specs=[spec, spec],
        out_specs=pl.BlockSpec((step, vocab), lambda i: (i, 0)),
        out_shape=jax.ShapeDtypeStruct((count, vocab), jnp.float32),
        cost_estimate=pl.CostEstimate(
            flops=2 * count * entries * vocab, bytes_accessed=4 * count * vocab, transcendentals=0
        ),
        name="marks",
    )(columns, probs)


def land_kernel(moved_ref, out_ref):
    out_ref[...] = moved_ref[...]


def gather_weight(weight):
    moved = lax.ppermute(weight.T, ("dp", "vocab"), SWAP_XY)
    hidden, half = moved.shape
    step = hidden // 4
    spec = pl.BlockSpec((step, half), lambda i: (i, 0))
    landed = pl.pallas_call(
        land_kernel,
        grid=(4,),
        in_specs=[spec],
        out_specs=spec,
        out_shape=jax.ShapeDtypeStruct(moved.shape, moved.dtype),
        cost_estimate=pl.CostEstimate(flops=0, bytes_accessed=4 * moved.size, transcendentals=0),
        name="land",
    )(moved)
    return lax.all_gather(landed, "dp", axis=0)


def layers(
    head_input,
    body_input,
    head_weight,
    gate_weight,
    up_weight,
    down_weight,
    tile_ids,
    tile_probs,
    tile_slot,
):
    shards = NY * NZ
    own_rows, width = head_input.shape
    slots, entries = tile_ids.shape
    vocab = head_weight.shape[0]
    count = shards * own_rows
    place = lax.axis_index("vocab")
    share = width // shards

    gate_full = gather_weight(gate_weight)
    up_full = gather_weight(up_weight)
    down_full = gather_weight(down_weight)

    tiles = width // 128
    quarter = width // NY
    shared = jnp.concatenate(
        [
            as_tiles(head_input),
            (tile_ids // RADIX).astype(jnp.bfloat16).reshape(-1, 128),
            (tile_ids % RADIX).astype(jnp.bfloat16).reshape(-1, 128),
            tile_probs.reshape(-1, 128),
        ],
        axis=0,
    )
    size = own_rows * tiles
    packed = jnp.concatenate(
        [replicate(shared, NY), as_tiles(body_input).reshape(NY, -1, 128)], axis=1
    )
    packed = jnp.broadcast_to(packed[:, None], (NY, NZ) + packed.shape[1:])
    packed = packed.reshape((shards,) + packed.shape[2:])
    arrived = exchange(packed)
    head_rows = from_tiles(arrived[:, :size], own_rows)
    body_rows = from_tiles(arrived[:, shared.shape[0] :], own_rows)
    store = (
        arrived[:, size : shared.shape[0]]
        .reshape(shards, 3, slots, entries)
        .transpose(0, 2, 1, 3)
        .reshape(shards * slots, 3 * entries)
    )
    chosen_slot = (
        tile_slot[:, None] == lax.broadcasted_iota(jnp.int32, (count, shards * slots), 1)
    ).astype(jnp.bfloat16)
    found = jnp.dot(chosen_slot, store, preferred_element_type=jnp.float32)
    row_ids = (found[:, :entries] * RADIX + found[:, entries : 2 * entries]).astype(jnp.int32)
    row_probs = found[:, 2 * entries :]
    tail_mass = 1.0 - jnp.sum(row_probs, axis=1, keepdims=True)
    marks = make_marks(row_ids - place * vocab, row_probs, vocab)
    picked = marks >= 0.0
    teacher = jnp.maximum(marks, 0.0)

    logits = jnp.einsum("rd,vd->rv", head_rows, head_weight, preferred_element_type=jnp.float32)
    local_max = jnp.max(logits, axis=1, keepdims=True)
    rest = jnp.where(picked, -1e30, logits)
    local_rest_max = jnp.max(rest, axis=1, keepdims=True)
    local_top = jnp.sum(jnp.where(picked, jnp.exp(logits - local_max), 0.0), axis=1, keepdims=True)
    local_rest = jnp.sum(
        jnp.where(picked, 0.0, jnp.exp(rest - local_rest_max)), axis=1, keepdims=True
    )
    stats = jnp.concatenate([local_max, local_rest_max, local_top, local_rest], axis=1).T
    maxima, rest_maxima, tops, rests = jnp.split(exchange(replicate(stats, shards)), 4, axis=1)
    row_max = jnp.max(maxima, axis=0)
    rest_max = jnp.max(rest_maxima, axis=0)
    top_sum = jnp.sum(tops * jnp.exp(maxima - row_max), axis=0)
    rest_sum = jnp.sum(rests * jnp.exp(rest_maxima - rest_max), axis=0)
    total = top_sum + rest_sum * jnp.exp(rest_max - row_max)
    row_max, rest_max, rest_sum, total, top_share = (
        value.reshape(count, 1) for value in (row_max, rest_max, rest_sum, total, top_sum / total)
    )
    student = jnp.exp(logits - row_max) / total
    spread = jnp.where(picked, 0.0, jnp.exp(rest - rest_max)) / rest_sum
    logit_grad = (
        LOSS_SCALE
        * (
            student * (1.0 - tail_mass)
            + jnp.where(picked, tail_mass * student - teacher, -tail_mass * top_share * spread)
        )
    ).astype(jnp.bfloat16)

    gate_part = wide(body_rows, gate_full)
    up_part = wide(body_rows, up_full)

    partial = head_blocks(logit_grad, head_weight).reshape(NY, NZ, count, share)
    over_y = add_blocks(exchange(partial, Y_GROUPS)).astype(jnp.bfloat16)
    head_own = add_blocks(exchange(over_y, Z_GROUPS)).astype(jnp.bfloat16)
    head_grad = (
        exchange(replicate(head_own, NZ), Z_GROUPS).transpose(1, 0, 2).reshape(count, quarter)
    )

    parts = jnp.stack([gate_part, up_part, wide(head_grad, down_full)], axis=1)
    gate_act, up_act, down_grad = add_blocks(exchange(parts, Y_GROUPS))
    sigma = 1.0 / (1.0 + jnp.exp(-gate_act))
    gate_grad = (down_grad * up_act * sigma * (1.0 + gate_act * (1.0 - sigma))).astype(jnp.bfloat16)
    up_grad = (down_grad * gate_act * sigma).astype(jnp.bfloat16)
    both = exchange(replicate(jnp.stack([gate_grad, up_grad]), NY), Y_GROUPS)
    pieces = branch_blocks(both[:, 0], both[:, 1], gate_full, up_full)
    summed = add_blocks(exchange(pieces, Z_GROUPS))
    return (head_own.astype(jnp.float32) + summed).astype(jnp.bfloat16)


def solution(mesh):
    return jax.shard_map(
        layers,
        mesh=mesh,
        in_specs=(
            P(("dp", "vocab"), None),
            P(("dp", "vocab"), None),
            P("vocab", None),
            P("dp", "vocab"),
            P("dp", "vocab"),
            P("dp", "vocab"),
            P(("dp", "vocab"), None),
            P(("dp", "vocab"), None),
            P("dp"),
        ),
        out_specs=P("dp", "vocab"),
        check_vma=False,
    )
```

```python
import jax
import jax.numpy as jnp
from jax import lax
from jax.experimental import pallas as pl
from jax.sharding import PartitionSpec as P


LOSS_SCALE = 1024
NX, NY, NZ, CORES = 4, 4, 8, 2
RADIX = 128

Y_GROUPS = [[y * NZ + z for y in range(NY)] for z in range(NZ)]
Z_GROUPS = [[y * NZ + z for z in range(NZ)] for y in range(NY)]
X_GROUPS = [[x * CORES + c for x in range(NX)] for c in range(CORES)]
YC_GROUPS = [
    [(x * CORES + c) * NY * NZ + y * NZ + z for y in range(NY) for c in range(CORES)]
    for x in range(NX)
    for z in range(NZ)
]


def turns(dy, dz):
    return [
        (y * NZ + z, (y + dy) % NY * NZ + (z + dz) % NZ) for y in range(NY) for z in range(NZ)
    ]


SWAP_XY = [
    (
        (x * CORES + c) * NY * NZ + y * NZ + z,
        (y * CORES + c) * NY * NZ + x * NZ + z,
    )
    for x in range(NX)
    for c in range(CORES)
    for y in range(NY)
    for z in range(NZ)
]
NT = (((1,), (1,)), ((), ()))
TN = (((0,), (0,)), ((), ()))


def exchange(blocks, groups=None, axis="vocab"):
    return lax.all_to_all(blocks, axis, 0, 0, axis_index_groups=groups)


def swap_xy(array):
    return lax.ppermute(array, ("dp", "vocab"), SWAP_XY)


def collect(block):
    def turn(value, dy, dz):
        return lax.ppermute(value, "vocab", turns(dy, dz))

    ahead, behind = turn(block[None], 0, -1), turn(block[None], 0, 1)
    near = jnp.concatenate([behind, block[None], ahead])
    line = jnp.concatenate([turn(near, 0, 3), near, turn(near[:2], 0, -3)])
    plane = jnp.concatenate([line, turn(line, -1, 0), turn(line, 1, 0), turn(line, 2, 0)])
    place = lax.axis_index("vocab")
    y, z = place // NZ, place % NZ
    along = jnp.array([-4, -3, -2, -1, 0, 1, 2, 3], jnp.int32)
    across = jnp.array([0, 1, -1, -2], jnp.int32)
    source = ((y + across) % NY)[:, None] * NZ + ((z + along) % NZ)[None, :]
    return plane, source.reshape(-1)


def replicate(block, copies):
    return jnp.broadcast_to(block[None], (copies,) + block.shape)


def as_tiles(rows):
    count, width = rows.shape
    return rows.reshape(count, width // 128, 128).transpose(1, 0, 2).reshape(-1, 128)


def from_tiles(blocks, rows):
    shards, size, lanes = blocks.shape
    blocks = blocks.reshape(shards, size // rows, rows, lanes).transpose(0, 2, 1, 3)
    return blocks.reshape(shards * rows, size // rows * lanes)


def add_blocks(blocks):
    return jnp.sum(blocks.astype(jnp.float32), axis=0)


def wide_kernel(rows_ref, weight_ref, *refs):
    out_ref = refs[-1]
    half = weight_ref.shape[2]
    total = lax.dot_general(
        weight_ref[0], rows_ref[:, :half], NT, preferred_element_type=jnp.float32
    )
    total += lax.dot_general(
        weight_ref[1], rows_ref[:, half:], NT, preferred_element_type=jnp.float32
    )
    out_ref[0, 0] = total.astype(out_ref.dtype)


def wide(rows, weight, slot, buffer=None):
    count = rows.shape[0]
    blocks, hidden, half = weight.shape
    parts = blocks // CORES
    in_specs = [
        pl.BlockSpec(rows.shape, lambda i: (0, 0)),
        pl.BlockSpec((CORES, hidden, half), lambda i: (i, 0, 0)),
    ]
    args = (rows, weight)
    if buffer is not None:
        in_specs.append(pl.BlockSpec(memory_space=pl.ANY))
        args += (buffer,)
    return pl.pallas_call(
        wide_kernel,
        grid=(parts,),
        in_specs=in_specs,
        out_specs=pl.BlockSpec((1, 1, hidden, count), lambda i: (i, slot, 0, 0)),
        out_shape=jax.ShapeDtypeStruct((parts, 3, hidden, count), jnp.bfloat16),
        input_output_aliases={} if buffer is None else {2: 0},
        cost_estimate=pl.CostEstimate(
            flops=2 * count * blocks * hidden * half,
            bytes_accessed=2 * (weight.size + rows.size),
            transcendentals=0,
        ),
        name="wide",
    )(*args)


def branch_kernel(act_ref, gate_weight_ref, up_weight_ref, out_ref):
    total = None
    for i in range(act_ref.shape[0]):
        for k, weight in enumerate((gate_weight_ref, up_weight_ref)):
            part = lax.dot_general(
                act_ref[i, k], weight[i, 0], TN, preferred_element_type=jnp.float32
            )
            total = part if total is None else total + part
    out_ref[0] = total.astype(out_ref.dtype)


def branch_blocks(acts, gate_weight, up_weight):
    parts, _, hidden, count = acts.shape
    half = gate_weight.shape[2]
    share = CORES * half // NZ
    per = half // share
    gate_weight = gate_weight.reshape(parts, CORES, hidden, half)
    up_weight = up_weight.reshape(parts, CORES, hidden, half)
    weight_spec = pl.BlockSpec((parts, 1, hidden, share), lambda i: (0, i // per, 0, i % per))
    return pl.pallas_call(
        branch_kernel,
        grid=(NZ,),
        in_specs=[pl.BlockSpec(acts.shape, lambda i: (0, 0, 0, 0)), weight_spec, weight_spec],
        out_specs=pl.BlockSpec((1, count, share), lambda i: (i, 0, 0)),
        out_shape=jax.ShapeDtypeStruct((NZ, count, share), jnp.bfloat16),
        cost_estimate=pl.CostEstimate(
            flops=4 * count * gate_weight.size,
            bytes_accessed=4 * gate_weight.size,
            transcendentals=0,
        ),
        name="branch",
    )(acts, gate_weight, up_weight)


def head_kernel(grad_ref, weight_ref, out_ref):
    for i in range(out_ref.shape[0]):
        share = out_ref.shape[2]
        out_ref[i] = jnp.dot(
            grad_ref[...],
            weight_ref[:, i * share : (i + 1) * share],
            preferred_element_type=jnp.float32,
        ).astype(out_ref.dtype)


def head_blocks(grad, weight):
    count, vocab = grad.shape
    width = weight.shape[1]
    parts = NY * NZ
    share = width // parts
    step = 4
    return pl.pallas_call(
        head_kernel,
        grid=(parts // step,),
        in_specs=[
            pl.BlockSpec(grad.shape, lambda i: (0, 0)),
            pl.BlockSpec((vocab, step * share), lambda i: (0, i)),
        ],
        out_specs=pl.BlockSpec((step, count, share), lambda i: (i, 0, 0)),
        out_shape=jax.ShapeDtypeStruct((parts, count, share), jnp.bfloat16),
        cost_estimate=pl.CostEstimate(
            flops=2 * count * weight.size,
            bytes_accessed=2 * weight.size,
            transcendentals=0,
        ),
        name="head",
    )(grad, weight)


def marks_kernel(columns_ref, probs_ref, out_ref):
    _, entries = columns_ref.shape
    lanes = lax.broadcasted_iota(jnp.int32, out_ref.shape, 1)
    columns = columns_ref[...]
    probs = probs_ref[...]
    marks = jnp.full(out_ref.shape, -1.0, jnp.float32)
    for k in range(entries):
        marks = jnp.where(lanes == columns[:, k : k + 1], probs[:, k : k + 1], marks)
    out_ref[...] = marks


def make_marks(columns, probs, vocab):
    count, entries = columns.shape
    step = 16
    spec = pl.BlockSpec((step, entries), lambda i: (i, 0))
    return pl.pallas_call(
        marks_kernel,
        grid=(count // step,),
        in_specs=[spec, spec],
        out_specs=pl.BlockSpec((step, vocab), lambda i: (i, 0)),
        out_shape=jax.ShapeDtypeStruct((count, vocab), jnp.float32),
        cost_estimate=pl.CostEstimate(
            flops=2 * count * entries * vocab, bytes_accessed=4 * count * vocab, transcendentals=0
        ),
        name="marks",
    )(columns, probs)


def gather_weight(weight):
    return lax.all_gather(weight.T, ("dp", "vocab"), axis=0, axis_index_groups=YC_GROUPS)


def layers(
    head_input,
    body_input,
    head_weight,
    gate_weight,
    up_weight,
    down_weight,
    tile_ids,
    tile_probs,
    tile_slot,
):
    shards = NY * NZ
    own_rows, width = head_input.shape
    slots, entries = tile_ids.shape
    vocab = head_weight.shape[0]
    count = shards * own_rows
    place = lax.axis_index("vocab")
    share = width // shards

    gate_full = gather_weight(gate_weight)
    up_full = gather_weight(up_weight)
    down_full = gather_weight(down_weight)

    quarter = width // NY
    head_tiles = as_tiles(head_input)
    size = head_tiles.shape[0]
    packed = jnp.concatenate(
        [replicate(head_tiles, NY), as_tiles(body_input).reshape(NY, -1, 128)], axis=1
    )
    packed = jnp.broadcast_to(packed[:, None], (NY, NZ) + packed.shape[1:])
    packed = packed.reshape((shards,) + packed.shape[2:])
    arrived = exchange(packed)
    head_rows = from_tiles(arrived[:, :size], own_rows)
    body_rows = swap_xy(from_tiles(arrived[:, size:], own_rows))

    tile = jnp.concatenate(
        [
            (tile_ids // RADIX).astype(jnp.bfloat16),
            (tile_ids % RADIX).astype(jnp.bfloat16),
            tile_probs,
        ],
        axis=1,
    )
    store, source = collect(tile)
    store = store.reshape(shards * slots, 3 * entries)
    store_slot = (source[:, None] * slots + jnp.arange(slots, dtype=jnp.int32)).reshape(1, -1)
    chosen_slot = (tile_slot[:, None] == store_slot).astype(jnp.bfloat16)
    found = jnp.dot(chosen_slot, store, preferred_element_type=jnp.float32)
    row_ids = (found[:, :entries] * RADIX + found[:, entries : 2 * entries]).astype(jnp.int32)
    row_probs = found[:, 2 * entries :]
    tail_mass = 1.0 - jnp.sum(row_probs, axis=1, keepdims=True)
    marks = make_marks(row_ids - place * vocab, row_probs, vocab)
    picked = marks >= 0.0
    teacher = jnp.maximum(marks, 0.0)

    logits = jnp.einsum("rd,vd->rv", head_rows, head_weight, preferred_element_type=jnp.float32)
    local_max = jnp.max(logits, axis=1, keepdims=True)
    rest = jnp.where(picked, -1e30, logits)
    local_rest_max = jnp.max(rest, axis=1, keepdims=True)
    local_top = jnp.sum(jnp.where(picked, jnp.exp(logits - local_max), 0.0), axis=1, keepdims=True)
    local_rest = jnp.sum(
        jnp.where(picked, 0.0, jnp.exp(rest - local_rest_max)), axis=1, keepdims=True
    )
    stats = jnp.concatenate([local_max, local_rest_max, local_top, local_rest], axis=1).T
    every = exchange(replicate(stats, shards))
    maxima, rest_maxima, tops, rests = jnp.split(every, 4, axis=1)
    row_max = jnp.max(maxima, axis=0)
    rest_max = jnp.max(rest_maxima, axis=0)
    top_sum = jnp.sum(tops * jnp.exp(maxima - row_max), axis=0)
    rest_sum = jnp.sum(rests * jnp.exp(rest_maxima - rest_max), axis=0)
    total = top_sum + rest_sum * jnp.exp(rest_max - row_max)
    row_max, rest_max, rest_sum, total, top_share = (
        value.reshape(count, 1) for value in (row_max, rest_max, rest_sum, total, top_sum / total)
    )
    student = jnp.exp(logits - row_max) / total
    spread = jnp.where(picked, 0.0, jnp.exp(rest - rest_max)) / rest_sum
    logit_grad = (
        LOSS_SCALE
        * (
            student * (1.0 - tail_mass)
            + jnp.where(picked, tail_mass * student - teacher, -tail_mass * top_share * spread)
        )
    ).astype(jnp.bfloat16)

    parts = wide(body_rows, gate_full, 0)
    parts = wide(body_rows, up_full, 1, parts)

    partial = head_blocks(logit_grad, head_weight).reshape(NY, NZ, count, share)
    arrived = exchange(partial, Y_GROUPS)
    over_y = add_blocks(arrived).astype(jnp.bfloat16)
    head_own = add_blocks(exchange(over_y, Z_GROUPS)).astype(jnp.bfloat16)
    head_own = swap_xy(head_own)
    head_grad = (
        exchange(replicate(head_own, NZ), Z_GROUPS).transpose(1, 0, 2).reshape(count, quarter)
    )

    parts = wide(head_grad, down_full, 2, parts)
    gate_act, up_act, down_grad = add_blocks(exchange(parts, X_GROUPS, "dp"))
    sigma = 1.0 / (1.0 + jnp.exp(-gate_act))
    gate_grad = (down_grad * up_act * sigma * (1.0 + gate_act * (1.0 - sigma))).astype(jnp.bfloat16)
    up_grad = (down_grad * gate_act * sigma).astype(jnp.bfloat16)
    both = exchange(replicate(jnp.stack([gate_grad, up_grad]), NX), X_GROUPS, "dp")
    summed = add_blocks(exchange(branch_blocks(both, gate_full, up_full), Z_GROUPS))
    return swap_xy((head_own.astype(jnp.float32) + summed).astype(jnp.bfloat16))


def solution(mesh):
    return jax.shard_map(
        layers,
        mesh=mesh,
        in_specs=(
            P(("dp", "vocab"), None),
            P(("dp", "vocab"), None),
            P("vocab", None),
            P("dp", "vocab"),
            P("dp", "vocab"),
            P("dp", "vocab"),
            P(("dp", "vocab"), None),
            P(("dp", "vocab"), None),
            P("dp"),
        ),
        out_specs=P("dp", "vocab"),
        check_vma=False,
    )
```

```python
import jax
import jax.numpy as jnp
from jax import lax
from jax.experimental import pallas as pl
from jax.experimental.pallas import tpu as pltpu
from jax.sharding import PartitionSpec as P


LOSS_SCALE = 1024
NX, NY, NZ, CORES = 4, 4, 8, 2
RADIX = 128

Y_GROUPS = [[y * NZ + z for y in range(NY)] for z in range(NZ)]
Z_GROUPS = [[y * NZ + z for z in range(NZ)] for y in range(NY)]
X_GROUPS = [[x * CORES + c for x in range(NX)] for c in range(CORES)]
YC_GROUPS = [
    [(x * CORES + c) * NY * NZ + y * NZ + z for y in range(NY) for c in range(CORES)]
    for x in range(NX)
    for z in range(NZ)
]

X_TURNS = {
    step: [(x * CORES + c, (x + step) % NX * CORES + c) for x in range(NX) for c in range(CORES)]
    for step in range(1, NX)
}
SWAP_XY = [
    (
        (x * CORES + c) * NY * NZ + y * NZ + z,
        (y * CORES + c) * NY * NZ + x * NZ + z,
    )
    for x in range(NX)
    for c in range(CORES)
    for y in range(NY)
    for z in range(NZ)
]
NT = (((1,), (1,)), ((), ()))
TN = (((0,), (0,)), ((), ()))


def exchange(blocks, groups=None, axis="vocab"):
    return lax.all_to_all(blocks, axis, 0, 0, axis_index_groups=groups)


def swap_xy(array):
    return lax.ppermute(array, ("dp", "vocab"), SWAP_XY)


def replicate(block, copies):
    return jnp.broadcast_to(block[None], (copies,) + block.shape)


def as_tiles(rows):
    count, width = rows.shape
    return rows.reshape(count, width // 128, 128).transpose(1, 0, 2).reshape(-1, 128)


def from_tiles(blocks, rows):
    shards, size, lanes = blocks.shape
    blocks = blocks.reshape(shards, size // rows, rows, lanes).transpose(0, 2, 1, 3)
    return blocks.reshape(shards * rows, size // rows * lanes)


def add_blocks(blocks):
    return jnp.sum(blocks.astype(jnp.float32), axis=0)


def wide_kernel(rows_ref, weight_ref, *refs):
    out_ref = refs[-1]
    half = weight_ref.shape[2]
    total = lax.dot_general(
        weight_ref[0], rows_ref[:, :half], NT, preferred_element_type=jnp.float32
    )
    total += lax.dot_general(
        weight_ref[1], rows_ref[:, half:], NT, preferred_element_type=jnp.float32
    )
    out_ref[0, 0] = total.astype(out_ref.dtype)


def wide(rows, weight, slot, entries, buffer=None):
    count = rows.shape[0]
    blocks, hidden, half = weight.shape
    parts = blocks // CORES
    in_specs = [
        pl.BlockSpec(rows.shape, lambda i: (0, 0)),
        pl.BlockSpec((CORES, hidden, half), lambda i: (i, 0, 0)),
    ]
    args = (rows, weight)
    if buffer is not None:
        in_specs.append(pl.BlockSpec(memory_space=pl.ANY))
        args += (buffer,)
    return pl.pallas_call(
        wide_kernel,
        grid=(parts,),
        in_specs=in_specs,
        out_specs=pl.BlockSpec((1, 1, hidden, count), lambda i: (i, slot, 0, 0)),
        out_shape=jax.ShapeDtypeStruct((parts, entries, hidden, count), jnp.bfloat16),
        input_output_aliases={} if buffer is None else {2: 0},
        cost_estimate=pl.CostEstimate(
            flops=2 * count * blocks * hidden * half,
            bytes_accessed=2 * (weight.size + rows.size),
            transcendentals=0,
        ),
        name="wide",
    )(*args)


def branch_kernel(act_ref, gate_weight_ref, up_weight_ref, out_ref):
    total = None
    for i in range(act_ref.shape[0]):
        for k, weight in enumerate((gate_weight_ref, up_weight_ref)):
            part = lax.dot_general(
                act_ref[i, k], weight[i, 0], TN, preferred_element_type=jnp.float32
            )
            total = part if total is None else total + part
    out_ref[0] = total.astype(out_ref.dtype)


def branch_blocks(acts, gate_weight, up_weight):
    parts, _, hidden, count = acts.shape
    half = gate_weight.shape[2]
    share = CORES * half // NZ
    per = half // share
    gate_weight = gate_weight.reshape(parts, CORES, hidden, half)
    up_weight = up_weight.reshape(parts, CORES, hidden, half)
    weight_spec = pl.BlockSpec((parts, 1, hidden, share), lambda i: (0, i // per, 0, i % per))
    return pl.pallas_call(
        branch_kernel,
        grid=(NZ,),
        in_specs=[pl.BlockSpec(acts.shape, lambda i: (0, 0, 0, 0)), weight_spec, weight_spec],
        out_specs=pl.BlockSpec((1, count, share), lambda i: (i, 0, 0)),
        out_shape=jax.ShapeDtypeStruct((NZ, count, share), jnp.bfloat16),
        cost_estimate=pl.CostEstimate(
            flops=4 * count * gate_weight.size,
            bytes_accessed=4 * gate_weight.size,
            transcendentals=0,
        ),
        name="branch",
    )(acts, gate_weight, up_weight)


def head_kernel(grad_ref, weight_ref, out_ref):
    for i in range(out_ref.shape[0]):
        share = out_ref.shape[2]
        out_ref[i] = jnp.dot(
            grad_ref[...],
            weight_ref[:, i * share : (i + 1) * share],
            preferred_element_type=jnp.float32,
        ).astype(out_ref.dtype)


def head_blocks(grad, weight):
    count, vocab = grad.shape
    width = weight.shape[1]
    parts = NY * NZ
    share = width // parts
    step = 4
    return pl.pallas_call(
        head_kernel,
        grid=(parts // step,),
        in_specs=[
            pl.BlockSpec(grad.shape, lambda i: (0, 0)),
            pl.BlockSpec((vocab, step * share), lambda i: (0, i)),
        ],
        out_specs=pl.BlockSpec((step, count, share), lambda i: (i, 0, 0)),
        out_shape=jax.ShapeDtypeStruct((parts, count, share), jnp.bfloat16),
        cost_estimate=pl.CostEstimate(
            flops=2 * count * weight.size,
            bytes_accessed=2 * weight.size,
            transcendentals=0,
        ),
        name="head",
    )(grad, weight)


def score_kernel(
    blocks_ref, low_ref, high_ref, columns_ref, probs_ref, logits_ref, marks_ref, low_sum, high_sum
):
    step = pl.program_id(0)
    shards, size, lanes = blocks_ref.shape
    both = 2 * logits_ref.shape[1]
    rows = jnp.concatenate(
        [
            blocks_ref[:, i * both : (i + 1) * both].reshape(shards * both, lanes)
            for i in range(size // both)
        ],
        axis=1,
    )
    for weight_ref, total in ((low_ref, low_sum), (high_ref, high_sum)):
        part = lax.dot_general(rows, weight_ref[...], NT, preferred_element_type=jnp.float32)
        total[...] = jnp.where(step == 0, 0.0, total[...]) + part
    entries = columns_ref.shape[1]
    places = lax.broadcasted_iota(jnp.int32, marks_ref.shape, 1)
    columns = columns_ref[...]
    probs = probs_ref[...]
    marks = jnp.full(marks_ref.shape, -1.0, jnp.float32)
    for k in range(entries):
        marks = jnp.where(places == columns[:, k : k + 1], probs[:, k : k + 1], marks)
    marks_ref[...] = marks

    @pl.when(step == pl.num_programs(0) - 1)
    def _():
        low = low_sum[...].reshape(shards, both, -1)
        high = high_sum[...].reshape(shards, both, -1)
        logits_ref[...] = low[:, : both // 2] + high[:, both // 2 :]


def score(blocks, weight, columns, probs):
    shards = blocks.shape[0]
    count, entries = columns.shape
    vocab, width = weight.shape
    own_rows = count // shards
    steps = 8
    chunk = width // 2 // steps
    size = chunk // 128 * 2 * own_rows
    band = pl.BlockSpec((count // steps, entries), lambda i: (i, 0))
    return pl.pallas_call(
        score_kernel,
        grid=(steps,),
        in_specs=[
            pl.BlockSpec((shards, size, 128), lambda i: (0, i, 0)),
            pl.BlockSpec((vocab, chunk), lambda i: (0, i)),
            pl.BlockSpec((vocab, chunk), lambda i: (0, i + steps)),
            band,
            band,
        ],
        out_specs=[
            pl.BlockSpec((shards, own_rows, vocab), lambda i: (0, 0, 0)),
            pl.BlockSpec((count // steps, vocab), lambda i: (i, 0)),
        ],
        out_shape=[
            jax.ShapeDtypeStruct((shards, own_rows, vocab), jnp.float32),
            jax.ShapeDtypeStruct((count, vocab), jnp.float32),
        ],
        scratch_shapes=[pltpu.VMEM((2 * count, vocab), jnp.float32)] * 2,
        cost_estimate=pl.CostEstimate(
            flops=2 * count * weight.size, bytes_accessed=2 * weight.size, transcendentals=0
        ),
        name="score",
    )(blocks, weight, weight, columns, probs)


def gather_weight(weight):
    return lax.all_gather(weight.T, ("dp", "vocab"), axis=0, axis_index_groups=YC_GROUPS)


def layers(
    head_input,
    body_input,
    head_weight,
    gate_weight,
    up_weight,
    down_weight,
    tile_ids,
    tile_probs,
    tile_slot,
):
    shards = NY * NZ
    own_rows, width = head_input.shape
    slots, entries = tile_ids.shape
    vocab = head_weight.shape[0]
    count = shards * own_rows
    place = lax.axis_index("vocab")
    share = width // shards

    gate_full = gather_weight(gate_weight)
    up_full = gather_weight(up_weight)
    down_full = gather_weight(down_weight)

    quarter = width // NY
    shared = jnp.concatenate(
        [
            head_input.reshape(own_rows, 2, -1, 128).transpose(2, 1, 0, 3).reshape(-1, 128),
            (tile_ids // RADIX).astype(jnp.bfloat16).reshape(-1, 128),
            (tile_ids % RADIX).astype(jnp.bfloat16).reshape(-1, 128),
            tile_probs.reshape(-1, 128),
        ],
        axis=0,
    )
    size, whole = own_rows * width // 128, shared.shape[0]
    packed = jnp.concatenate(
        [replicate(shared, NY), as_tiles(body_input).reshape(NY, -1, 128)], axis=1
    )
    packed = jnp.broadcast_to(packed[:, None], (NY, NZ) + packed.shape[1:])
    packed = packed.reshape((shards,) + packed.shape[2:])
    arrived = exchange(packed)
    body_rows = from_tiles(swap_xy(arrived[:, whole:]), own_rows)
    store = (
        arrived[:, size:whole]
        .reshape(shards, 3, slots, entries)
        .transpose(0, 2, 1, 3)
        .reshape(shards * slots, 3 * entries)
    )
    chosen_slot = (
        tile_slot[:, None] == lax.broadcasted_iota(jnp.int32, (count, shards * slots), 1)
    ).astype(jnp.bfloat16)
    found = jnp.dot(chosen_slot, store, preferred_element_type=jnp.float32)
    row_ids = (found[:, :entries] * RADIX + found[:, entries : 2 * entries]).astype(jnp.int32)
    row_probs = found[:, 2 * entries :]
    tail_mass = 1.0 - jnp.sum(row_probs, axis=1, keepdims=True)
    logits, marks = score(arrived, head_weight, row_ids - place * vocab, row_probs)
    logits = logits.reshape(count, vocab)
    picked = marks >= 0.0
    teacher = jnp.maximum(marks, 0.0)

    local_max = jnp.max(logits, axis=1, keepdims=True)
    rest = jnp.where(picked, -1e30, logits)
    local_rest_max = jnp.max(rest, axis=1, keepdims=True)
    local_top = jnp.sum(jnp.where(picked, jnp.exp(logits - local_max), 0.0), axis=1, keepdims=True)
    local_rest = jnp.sum(
        jnp.where(picked, 0.0, jnp.exp(rest - local_rest_max)), axis=1, keepdims=True
    )
    stats = jnp.concatenate([local_max, local_rest_max, local_top, local_rest], axis=1).T
    every = exchange(replicate(stats, shards))
    maxima, rest_maxima, tops, rests = jnp.split(every, 4, axis=1)
    row_max = jnp.max(maxima, axis=0)
    rest_max = jnp.max(rest_maxima, axis=0)
    top_sum = jnp.sum(tops * jnp.exp(maxima - row_max), axis=0)
    rest_sum = jnp.sum(rests * jnp.exp(rest_maxima - rest_max), axis=0)
    total = top_sum + rest_sum * jnp.exp(rest_max - row_max)
    row_max, rest_max, rest_sum, total, top_share = (
        value.reshape(count, 1) for value in (row_max, rest_max, rest_sum, total, top_sum / total)
    )
    student = jnp.exp(logits - row_max) / total
    spread = jnp.where(picked, 0.0, jnp.exp(rest - rest_max)) / rest_sum
    logit_grad = (
        LOSS_SCALE
        * (
            student * (1.0 - tail_mass)
            + jnp.where(picked, tail_mass * student - teacher, -tail_mass * top_share * spread)
        )
    ).astype(jnp.bfloat16)

    acts = wide(body_rows, gate_full, 0, 2)
    acts = wide(body_rows, up_full, 1, 2, acts)
    chip = lax.axis_index("dp") // CORES

    def turn_acts(step):
        block = lax.dynamic_index_in_dim(acts, (chip + step) % NX, 0, keepdims=False)
        return lax.ppermute(block, "dp", X_TURNS[step]) if step else block

    gathered = [turn_acts(step) for step in range(NX)]
    gate_act, up_act = sum(block.astype(jnp.float32) for block in gathered)

    partial = head_blocks(logit_grad, head_weight).reshape(NY, NZ, count, share)
    arrived = exchange(partial, Y_GROUPS)
    over_y = add_blocks(arrived).astype(jnp.bfloat16)
    arrived = exchange(over_y, Z_GROUPS)
    head_own = add_blocks(arrived).astype(jnp.bfloat16)
    head_own = swap_xy(head_own)
    head_grad = (
        exchange(replicate(head_own, NZ), Z_GROUPS).transpose(1, 0, 2).reshape(count, quarter)
    )

    down_grad = add_blocks(exchange(wide(head_grad, down_full, 0, 1)[:, 0], X_GROUPS, "dp"))
    sigma = 1.0 / (1.0 + jnp.exp(-gate_act))
    gate_grad = (down_grad * up_act * sigma * (1.0 + gate_act * (1.0 - sigma))).astype(jnp.bfloat16)
    up_grad = (down_grad * gate_act * sigma).astype(jnp.bfloat16)
    both = exchange(replicate(jnp.stack([gate_grad, up_grad]), NX), X_GROUPS, "dp")
    summed = add_blocks(exchange(branch_blocks(both, gate_full, up_full), Z_GROUPS))
    return swap_xy((head_own.astype(jnp.float32) + summed).astype(jnp.bfloat16))


def solution(mesh):
    return jax.shard_map(
        layers,
        mesh=mesh,
        in_specs=(
            P(("dp", "vocab"), None),
            P(("dp", "vocab"), None),
            P("vocab", None),
            P("dp", "vocab"),
            P("dp", "vocab"),
            P("dp", "vocab"),
            P(("dp", "vocab"), None),
            P(("dp", "vocab"), None),
            P("dp"),
        ),
        out_specs=P("dp", "vocab"),
        check_vma=False,
    )
```

```python
import jax
import jax.numpy as jnp
from jax import lax
from jax.experimental import pallas as pl
from jax.experimental.pallas import tpu as pltpu
from jax.sharding import PartitionSpec as P


LOSS_SCALE = 1024
NX, NY, NZ, CORES = 4, 4, 8, 2
RADIX = 128

Y_GROUPS = [[y * NZ + z for y in range(NY)] for z in range(NZ)]
Z_GROUPS = [[y * NZ + z for z in range(NZ)] for y in range(NY)]
X_GROUPS = [[x * CORES + c for x in range(NX)] for c in range(CORES)]
YC_GROUPS = [
    [(x * CORES + c) * NY * NZ + y * NZ + z for y in range(NY) for c in range(CORES)]
    for x in range(NX)
    for z in range(NZ)
]

X_TURNS = {
    step: [(x * CORES + c, (x + step) % NX * CORES + c) for x in range(NX) for c in range(CORES)]
    for step in range(1, NX)
}
XZ_GROUPS = [
    [(x * CORES + c) * NY * NZ + y * NZ + z for x in range(NX) for z in range(NZ)]
    for c in range(CORES)
    for y in range(NY)
]
X_TURNS = {
    step: [(x * CORES + c, (x + step) % NX * CORES + c) for x in range(NX) for c in range(CORES)]
    for step in range(1, NX)
}
NT = (((1,), (1,)), ((), ()))
TN = (((0,), (0,)), ((), ()))


def exchange(blocks, groups=None, axis="vocab"):
    return lax.all_to_all(blocks, axis, 0, 0, axis_index_groups=groups)


def replicate(block, copies):
    return jnp.broadcast_to(block[None], (copies,) + block.shape)


def as_tiles(rows):
    count, width = rows.shape
    return rows.reshape(count, width // 128, 128).transpose(1, 0, 2).reshape(-1, 128)


def from_tiles(blocks, rows):
    shards, size, lanes = blocks.shape
    blocks = blocks.reshape(shards, size // rows, rows, lanes).transpose(0, 2, 1, 3)
    return blocks.reshape(shards * rows, size // rows * lanes)


def add_blocks(blocks):
    return jnp.sum(blocks.astype(jnp.float32), axis=0)


def wide_kernel(rows_ref, weight_ref, *refs):
    out_ref = refs[-1]
    half = weight_ref.shape[2]
    total = lax.dot_general(
        weight_ref[0], rows_ref[:, :half], NT, preferred_element_type=jnp.float32
    )
    total += lax.dot_general(
        weight_ref[1], rows_ref[:, half:], NT, preferred_element_type=jnp.float32
    )
    out_ref[0, 0] = total.astype(out_ref.dtype)


def wide(rows, weight, slot, entries, buffer=None):
    count = rows.shape[0]
    blocks, hidden, half = weight.shape
    parts = blocks // CORES
    in_specs = [
        pl.BlockSpec(rows.shape, lambda i: (0, 0)),
        pl.BlockSpec((CORES, hidden, half), lambda i: (i, 0, 0)),
    ]
    args = (rows, weight)
    if buffer is not None:
        in_specs.append(pl.BlockSpec(memory_space=pl.ANY))
        args += (buffer,)
    return pl.pallas_call(
        wide_kernel,
        grid=(parts,),
        in_specs=in_specs,
        out_specs=pl.BlockSpec((1, 1, hidden, count), lambda i: (i, slot, 0, 0)),
        out_shape=jax.ShapeDtypeStruct((parts, entries, hidden, count), jnp.bfloat16),
        input_output_aliases={} if buffer is None else {2: 0},
        cost_estimate=pl.CostEstimate(
            flops=2 * count * blocks * hidden * half,
            bytes_accessed=2 * (weight.size + rows.size),
            transcendentals=0,
        ),
        name="wide",
    )(*args)


def branch_kernel(place_ref, act_ref, gate_weight_ref, up_weight_ref, extra_ref, out_ref):
    total = None
    for i in range(act_ref.shape[0]):
        for k, weight in enumerate((gate_weight_ref, up_weight_ref)):
            part = lax.dot_general(
                act_ref[i, k], weight[i, 0], TN, preferred_element_type=jnp.float32
            )
            total = part if total is None else total + part
    total += jnp.where(pl.program_id(0) == place_ref[0], extra_ref[...].astype(jnp.float32), 0.0)
    parts, _, rows, share = out_ref.shape
    out_ref[:, 0] = total.reshape(parts, rows, share).astype(out_ref.dtype)


def branch_blocks(acts, gate_weight, up_weight, extra, place):
    parts, _, hidden, count = acts.shape
    half = gate_weight.shape[2]
    share = CORES * half // NZ
    per = half // share
    gate_weight = gate_weight.reshape(parts, CORES, hidden, half)
    up_weight = up_weight.reshape(parts, CORES, hidden, half)
    weight_spec = pl.BlockSpec((parts, 1, hidden, share), lambda i: (0, i // per, 0, i % per))
    return pl.pallas_call(
        branch_kernel,
        grid=(NZ,),
        in_specs=[
            pl.BlockSpec(memory_space=pltpu.SMEM),
            pl.BlockSpec(acts.shape, lambda i: (0, 0, 0, 0)),
            weight_spec,
            weight_spec,
            pl.BlockSpec(extra.shape, lambda i: (0, 0)),
        ],
        out_specs=pl.BlockSpec((NX, 1, count // NX, share), lambda i: (0, i, 0, 0)),
        out_shape=jax.ShapeDtypeStruct((NX, NZ, count // NX, share), jnp.bfloat16),
        cost_estimate=pl.CostEstimate(
            flops=4 * count * gate_weight.size,
            bytes_accessed=4 * gate_weight.size,
            transcendentals=0,
        ),
        name="branch",
    )(place, acts, gate_weight, up_weight, extra)


def head_kernel(grad_ref, weight_ref, out_ref):
    quarters, steps, rows, share = out_ref.shape
    for i in range(steps):
        part = jnp.dot(
            grad_ref[...],
            weight_ref[:, i * share : (i + 1) * share],
            preferred_element_type=jnp.float32,
        )
        out_ref[:, i] = part.reshape(quarters, rows, share).astype(out_ref.dtype)


def head_blocks(grad, weight):
    count, vocab = grad.shape
    width = weight.shape[1]
    parts = NX * NZ
    share = width // parts
    step = 4
    return pl.pallas_call(
        head_kernel,
        grid=(parts // step,),
        in_specs=[
            pl.BlockSpec(grad.shape, lambda i: (0, 0)),
            pl.BlockSpec((vocab, step * share), lambda i: (0, i)),
        ],
        out_specs=pl.BlockSpec((NY, step, count // NY, share), lambda i: (0, i, 0, 0)),
        out_shape=jax.ShapeDtypeStruct((NY, parts, count // NY, share), jnp.bfloat16),
        cost_estimate=pl.CostEstimate(
            flops=2 * count * weight.size,
            bytes_accessed=2 * weight.size,
            transcendentals=0,
        ),
        name="head",
    )(grad, weight)


def score_kernel(
    blocks_ref, low_ref, high_ref, columns_ref, probs_ref, logits_ref, marks_ref, low_sum, high_sum
):
    step = pl.program_id(0)
    shards, size, lanes = blocks_ref.shape
    both = 2 * logits_ref.shape[1]
    rows = jnp.concatenate(
        [
            blocks_ref[:, i * both : (i + 1) * both].reshape(shards * both, lanes)
            for i in range(size // both)
        ],
        axis=1,
    )
    for weight_ref, total in ((low_ref, low_sum), (high_ref, high_sum)):
        part = lax.dot_general(rows, weight_ref[...], NT, preferred_element_type=jnp.float32)
        total[...] = jnp.where(step == 0, 0.0, total[...]) + part
    entries = columns_ref.shape[1]
    places = lax.broadcasted_iota(jnp.int32, marks_ref.shape, 1)
    columns = columns_ref[...]
    probs = probs_ref[...]
    marks = jnp.full(marks_ref.shape, -1.0, jnp.float32)
    for k in range(entries):
        marks = jnp.where(places == columns[:, k : k + 1], probs[:, k : k + 1], marks)
    marks_ref[...] = marks

    @pl.when(step == pl.num_programs(0) - 1)
    def _():
        low = low_sum[...].reshape(shards, both, -1)
        high = high_sum[...].reshape(shards, both, -1)
        logits_ref[...] = low[:, : both // 2] + high[:, both // 2 :]


def score(blocks, weight, columns, probs):
    shards = blocks.shape[0]
    count, entries = columns.shape
    vocab, width = weight.shape
    own_rows = count // shards
    steps = 8
    chunk = width // 2 // steps
    size = chunk // 128 * 2 * own_rows
    band = pl.BlockSpec((count // steps, entries), lambda i: (i, 0))
    return pl.pallas_call(
        score_kernel,
        grid=(steps,),
        in_specs=[
            pl.BlockSpec((shards, size, 128), lambda i: (0, i, 0)),
            pl.BlockSpec((vocab, chunk), lambda i: (0, i)),
            pl.BlockSpec((vocab, chunk), lambda i: (0, i + steps)),
            band,
            band,
        ],
        out_specs=[
            pl.BlockSpec((shards, own_rows, vocab), lambda i: (0, 0, 0)),
            pl.BlockSpec((count // steps, vocab), lambda i: (i, 0)),
        ],
        out_shape=[
            jax.ShapeDtypeStruct((shards, own_rows, vocab), jnp.float32),
            jax.ShapeDtypeStruct((count, vocab), jnp.float32),
        ],
        scratch_shapes=[pltpu.VMEM((2 * count, vocab), jnp.float32)] * 2,
        cost_estimate=pl.CostEstimate(
            flops=2 * count * weight.size, bytes_accessed=2 * weight.size, transcendentals=0
        ),
        name="score",
    )(blocks, weight, weight, columns, probs)


def gather_weight(weight):
    return lax.all_gather(weight.T, ("dp", "vocab"), axis=0, axis_index_groups=YC_GROUPS)


def layers(
    head_input,
    body_input,
    head_weight,
    gate_weight,
    up_weight,
    down_weight,
    tile_ids,
    tile_probs,
    tile_slot,
):
    shards = NY * NZ
    own_rows, width = head_input.shape
    slots, entries = tile_ids.shape
    vocab = head_weight.shape[0]
    count = shards * own_rows
    place = lax.axis_index("vocab")
    share = width // shards

    gate_full = gather_weight(gate_weight)
    up_full = gather_weight(up_weight)
    down_full = gather_weight(down_weight)

    quarter = width // NX
    packed = jnp.concatenate(
        [
            head_input.reshape(own_rows, 2, -1, 128).transpose(2, 1, 0, 3).reshape(-1, 128),
            (tile_ids // RADIX).astype(jnp.bfloat16).reshape(-1, 128),
            (tile_ids % RADIX).astype(jnp.bfloat16).reshape(-1, 128),
            tile_probs.reshape(-1, 128),
        ],
        axis=0,
    )
    size, whole = own_rows * width // 128, packed.shape[0]
    arrived = exchange(replicate(packed, shards))

    body_tiles = as_tiles(body_input).reshape(NX, 1, -1, 128)
    body_tiles = jnp.broadcast_to(body_tiles, (NX, NZ) + body_tiles.shape[2:])
    body_tiles = exchange(
        body_tiles.reshape((NX * NZ,) + body_tiles.shape[2:]), XZ_GROUPS, ("dp", "vocab")
    )
    body_rows = from_tiles(body_tiles, own_rows)
    store = (
        arrived[:, size:whole]
        .reshape(shards, 3, slots, entries)
        .transpose(0, 2, 1, 3)
        .reshape(shards * slots, 3 * entries)
    )
    chosen_slot = (
        tile_slot[:, None] == lax.broadcasted_iota(jnp.int32, (count, shards * slots), 1)
    ).astype(jnp.bfloat16)
    found = jnp.dot(chosen_slot, store, preferred_element_type=jnp.float32)
    row_ids = (found[:, :entries] * RADIX + found[:, entries : 2 * entries]).astype(jnp.int32)
    row_probs = found[:, 2 * entries :]
    tail_mass = 1.0 - jnp.sum(row_probs, axis=1, keepdims=True)
    logits, marks = score(arrived, head_weight, row_ids - place * vocab, row_probs)
    logits = logits.reshape(count, vocab)
    picked = marks >= 0.0
    teacher = jnp.maximum(marks, 0.0)

    local_max = jnp.max(logits, axis=1, keepdims=True)
    rest = jnp.where(picked, -1e30, logits)
    local_rest_max = jnp.max(rest, axis=1, keepdims=True)
    local_top = jnp.sum(jnp.where(picked, jnp.exp(logits - local_max), 0.0), axis=1, keepdims=True)
    local_rest = jnp.sum(
        jnp.where(picked, 0.0, jnp.exp(rest - local_rest_max)), axis=1, keepdims=True
    )
    stats = jnp.concatenate([local_max, local_rest_max, local_top, local_rest], axis=1).T
    every = exchange(replicate(stats, shards))
    maxima, rest_maxima, tops, rests = jnp.split(every, 4, axis=1)
    row_max = jnp.max(maxima, axis=0)
    rest_max = jnp.max(rest_maxima, axis=0)
    top_sum = jnp.sum(tops * jnp.exp(maxima - row_max), axis=0)
    rest_sum = jnp.sum(rests * jnp.exp(rest_maxima - rest_max), axis=0)
    total = top_sum + rest_sum * jnp.exp(rest_max - row_max)
    row_max, rest_max, rest_sum, total, top_share = (
        value.reshape(count, 1) for value in (row_max, rest_max, rest_sum, total, top_sum / total)
    )
    student = jnp.exp(logits - row_max) / total
    spread = jnp.where(picked, 0.0, jnp.exp(rest - rest_max)) / rest_sum
    logit_grad = (
        LOSS_SCALE
        * (
            student * (1.0 - tail_mass)
            + jnp.where(picked, tail_mass * student - teacher, -tail_mass * top_share * spread)
        )
    ).astype(jnp.bfloat16)

    acts = wide(body_rows, gate_full, 0, 2)
    acts = wide(body_rows, up_full, 1, 2, acts)
    chip = lax.axis_index("dp") // CORES

    def turn_acts(step):
        block = lax.dynamic_index_in_dim(acts, (chip + step) % NX, 0, keepdims=False)
        return lax.ppermute(block, "dp", X_TURNS[step]) if step else block

    gathered = [turn_acts(step) for step in range(NX)]
    gate_act, up_act = sum(block.astype(jnp.float32) for block in gathered)

    arrived = exchange(head_blocks(logit_grad, head_weight), Y_GROUPS)
    over_y = add_blocks(arrived).astype(jnp.bfloat16)
    arrived = exchange(over_y, XZ_GROUPS, ("dp", "vocab"))
    head_own = jnp.sum(
        arrived.reshape((NX, NZ) + arrived.shape[1:]).astype(jnp.float32), axis=1
    ).astype(jnp.bfloat16)
    head_own = head_own.reshape(count, share)
    head_grad = (
        exchange(replicate(head_own, NZ), Z_GROUPS).transpose(1, 0, 2).reshape(count, quarter)
    )

    down_grad = add_blocks(exchange(wide(head_grad, down_full, 0, 1)[:, 0], X_GROUPS, "dp"))
    sigma = 1.0 / (1.0 + jnp.exp(-gate_act))
    gate_grad = (down_grad * up_act * sigma * (1.0 + gate_act * (1.0 - sigma))).astype(jnp.bfloat16)
    up_grad = (down_grad * gate_act * sigma).astype(jnp.bfloat16)
    both = exchange(replicate(jnp.stack([gate_grad, up_grad]), NX), X_GROUPS, "dp")
    pieces = branch_blocks(both, gate_full, up_full, head_own, (place % NZ).reshape(1))
    arrived = exchange(
        pieces.reshape((NX * NZ,) + pieces.shape[2:]), XZ_GROUPS, ("dp", "vocab")
    )
    grads = jnp.sum(arrived.reshape((NX, NZ) + arrived.shape[1:]).astype(jnp.float32), axis=1)
    return exchange(grads.astype(jnp.bfloat16), Y_GROUPS).reshape(count, share)


def solution(mesh):
    return jax.shard_map(
        layers,
        mesh=mesh,
        in_specs=(
            P(("dp", "vocab"), None),
            P(("dp", "vocab"), None),
            P("vocab", None),
            P("dp", "vocab"),
            P("dp", "vocab"),
            P("dp", "vocab"),
            P(("dp", "vocab"), None),
            P(("dp", "vocab"), None),
            P("dp"),
        ),
        out_specs=P("dp", "vocab"),
        check_vma=False,
    )
```

```python
import jax
import jax.numpy as jnp
from jax import lax
from jax.experimental import pallas as pl
from jax.experimental.pallas import tpu as pltpu
from jax.sharding import PartitionSpec as P


LOSS_SCALE = 1024
NX, NY, NZ, CORES = 4, 4, 8, 2
RADIX = 128

Y_GROUPS = [[y * NZ + z for y in range(NY)] for z in range(NZ)]
Z_GROUPS = [[y * NZ + z for z in range(NZ)] for y in range(NY)]
X_GROUPS = [[x * CORES + c for x in range(NX)] for c in range(CORES)]
YC_GROUPS = [
    [(x * CORES + c) * NY * NZ + y * NZ + z for y in range(NY) for c in range(CORES)]
    for x in range(NX)
    for z in range(NZ)
]

Y_TURNS = {
    step: [
        (y * NZ + z, (y + step) % NY * NZ + z) for y in range(NY) for z in range(NZ)
    ]
    for step in (1, -1)
}
LINES = (0, -1, 1, 2)
X_TURNS = {
    step: [(x * CORES + c, (x + step) % NX * CORES + c) for x in range(NX) for c in range(CORES)]
    for step in range(1, NX)
}
XZ_GROUPS = [
    [(x * CORES + c) * NY * NZ + y * NZ + z for x in range(NX) for z in range(NZ)]
    for c in range(CORES)
    for y in range(NY)
]
Y_TURNS = {
    step: [
        (y * NZ + z, (y + step) % NY * NZ + z) for y in range(NY) for z in range(NZ)
    ]
    for step in (1, -1)
}
LINES = (0, -1, 1, 2)
X_TURNS = {
    step: [(x * CORES + c, (x + step) % NX * CORES + c) for x in range(NX) for c in range(CORES)]
    for step in range(1, NX)
}
NT = (((1,), (1,)), ((), ()))
TN = (((0,), (0,)), ((), ()))


def exchange(blocks, groups=None, axis="vocab"):
    return lax.all_to_all(blocks, axis, 0, 0, axis_index_groups=groups)


def replicate(block, copies):
    return jnp.broadcast_to(block[None], (copies,) + block.shape)


def as_tiles(rows):
    count, width = rows.shape
    return rows.reshape(count, width // 128, 128).transpose(1, 0, 2).reshape(-1, 128)


def from_tiles(blocks, rows):
    shards, size, lanes = blocks.shape
    blocks = blocks.reshape(shards, size // rows, rows, lanes).transpose(0, 2, 1, 3)
    return blocks.reshape(shards * rows, size // rows * lanes)


def add_blocks(blocks):
    return jnp.sum(blocks.astype(jnp.float32), axis=0)


def wide_kernel(rows_ref, weight_ref, *refs):
    out_ref = refs[-1]
    half = weight_ref.shape[2]
    total = lax.dot_general(
        weight_ref[0], rows_ref[:, :half], NT, preferred_element_type=jnp.float32
    )
    total += lax.dot_general(
        weight_ref[1], rows_ref[:, half:], NT, preferred_element_type=jnp.float32
    )
    out_ref[0, 0] = total.astype(out_ref.dtype)


def wide(rows, weight, slot, entries, buffer=None):
    count = rows.shape[0]
    blocks, hidden, half = weight.shape
    parts = blocks // CORES
    in_specs = [
        pl.BlockSpec(rows.shape, lambda i: (0, 0)),
        pl.BlockSpec((CORES, hidden, half), lambda i: (i, 0, 0)),
    ]
    args = (rows, weight)
    if buffer is not None:
        in_specs.append(pl.BlockSpec(memory_space=pl.ANY))
        args += (buffer,)
    return pl.pallas_call(
        wide_kernel,
        grid=(parts,),
        in_specs=in_specs,
        out_specs=pl.BlockSpec((1, 1, hidden, count), lambda i: (i, slot, 0, 0)),
        out_shape=jax.ShapeDtypeStruct((parts, entries, hidden, count), jnp.bfloat16),
        input_output_aliases={} if buffer is None else {2: 0},
        cost_estimate=pl.CostEstimate(
            flops=2 * count * blocks * hidden * half,
            bytes_accessed=2 * (weight.size + rows.size),
            transcendentals=0,
        ),
        name="wide",
    )(*args)


def branch_kernel(place_ref, act_ref, gate_weight_ref, up_weight_ref, extra_ref, out_ref):
    total = None
    for i in range(act_ref.shape[0]):
        for k, weight in enumerate((gate_weight_ref, up_weight_ref)):
            part = lax.dot_general(
                act_ref[i, k], weight[i, 0], TN, preferred_element_type=jnp.float32
            )
            total = part if total is None else total + part
    total += jnp.where(pl.program_id(0) == place_ref[0], extra_ref[...].astype(jnp.float32), 0.0)
    parts, _, rows, share = out_ref.shape
    out_ref[:, 0] = total.reshape(parts, rows, share).astype(out_ref.dtype)


def branch_blocks(acts, gate_weight, up_weight, extra, place):
    parts, _, hidden, count = acts.shape
    half = gate_weight.shape[2]
    share = CORES * half // NZ
    per = half // share
    gate_weight = gate_weight.reshape(parts, CORES, hidden, half)
    up_weight = up_weight.reshape(parts, CORES, hidden, half)
    weight_spec = pl.BlockSpec((parts, 1, hidden, share), lambda i: (0, i // per, 0, i % per))
    return pl.pallas_call(
        branch_kernel,
        grid=(NZ,),
        in_specs=[
            pl.BlockSpec(memory_space=pltpu.SMEM),
            pl.BlockSpec(acts.shape, lambda i: (0, 0, 0, 0)),
            weight_spec,
            weight_spec,
            pl.BlockSpec(extra.shape, lambda i: (0, 0)),
        ],
        out_specs=pl.BlockSpec((NX, 1, count // NX, share), lambda i: (0, i, 0, 0)),
        out_shape=jax.ShapeDtypeStruct((NX, NZ, count // NX, share), jnp.bfloat16),
        cost_estimate=pl.CostEstimate(
            flops=4 * count * gate_weight.size,
            bytes_accessed=4 * gate_weight.size,
            transcendentals=0,
        ),
        name="branch",
    )(place, acts, gate_weight, up_weight, extra)


def head_kernel(grad_ref, weight_ref, out_ref):
    quarters, steps, rows, share = out_ref.shape
    for i in range(steps):
        part = jnp.dot(
            grad_ref[...],
            weight_ref[:, i * share : (i + 1) * share],
            preferred_element_type=jnp.float32,
        )
        out_ref[:, i] = part.reshape(quarters, rows, share).astype(out_ref.dtype)


def head_blocks(grad, weight):
    count, vocab = grad.shape
    width = weight.shape[1]
    parts = NX * NZ
    share = width // parts
    step = 4
    return pl.pallas_call(
        head_kernel,
        grid=(parts // step,),
        in_specs=[
            pl.BlockSpec(grad.shape, lambda i: (0, 0)),
            pl.BlockSpec((vocab, step * share), lambda i: (0, i)),
        ],
        out_specs=pl.BlockSpec((NY, step, count // NY, share), lambda i: (0, i, 0, 0)),
        out_shape=jax.ShapeDtypeStruct((NY, parts, count // NY, share), jnp.bfloat16),
        cost_estimate=pl.CostEstimate(
            flops=2 * count * weight.size,
            bytes_accessed=2 * weight.size,
            transcendentals=0,
        ),
        name="head",
    )(grad, weight)


def score_kernel(place_ref, *refs):
    *block_refs, low_ref, high_ref, columns_ref, probs_ref = refs[:-4]
    logits_ref, marks_ref, low_sum, high_sum = refs[-4:]
    step = pl.program_id(0)
    both = 2 * logits_ref.shape[2]

    def tile(block_ref, i):
        shards, _, lanes = block_ref.shape
        return block_ref[:, i * both : (i + 1) * both].reshape(shards * both, lanes)

    rows = jnp.concatenate(
        [
            jnp.concatenate([tile(block_ref, i) for block_ref in block_refs], axis=0)
            for i in range(block_refs[0].shape[1] // both)
        ],
        axis=1,
    )
    for weight_ref, total in ((low_ref, low_sum), (high_ref, high_sum)):
        part = lax.dot_general(rows, weight_ref[...], NT, preferred_element_type=jnp.float32)
        total[...] = jnp.where(step == 0, 0.0, total[...]) + part
    entries = columns_ref.shape[1]
    places = lax.broadcasted_iota(jnp.int32, marks_ref.shape, 1)
    columns = columns_ref[...]
    probs = probs_ref[...]
    marks = jnp.full(marks_ref.shape, -1.0, jnp.float32)
    for k in range(entries):
        marks = jnp.where(places == columns[:, k : k + 1], probs[:, k : k + 1], marks)
    marks_ref[...] = marks

    @pl.when(step == pl.num_programs(0) - 1)
    def _():
        shards = NY * NZ
        low = low_sum[...].reshape(shards, both, -1)
        high = high_sum[...].reshape(shards, both, -1)
        logits = low[:, : both // 2] + high[:, both // 2 :]
        for i, line in enumerate(LINES):
            logits_ref[lax.rem(place_ref[0] + line + NY, NY)] = logits[i * NZ : (i + 1) * NZ]


def score(place, blocks, weight, columns, probs):
    count, entries = columns.shape
    vocab, width = weight.shape
    own_rows = count // (NY * NZ)
    steps = 8
    chunk = width // 2 // steps
    size = chunk // 128 * 2 * own_rows
    band = pl.BlockSpec((count // steps, entries), lambda i: (i, 0))
    return pl.pallas_call(
        score_kernel,
        grid=(steps,),
        in_specs=[pl.BlockSpec(memory_space=pltpu.SMEM)]
        + [pl.BlockSpec((block.shape[0], size, 128), lambda i: (0, i, 0)) for block in blocks]
        + [
            pl.BlockSpec((vocab, chunk), lambda i: (0, i)),
            pl.BlockSpec((vocab, chunk), lambda i: (0, i + steps)),
            band,
            band,
        ],
        out_specs=[
            pl.BlockSpec((NY, NZ, own_rows, vocab), lambda i: (0, 0, 0, 0)),
            pl.BlockSpec((count // steps, vocab), lambda i: (i, 0)),
        ],
        out_shape=[
            jax.ShapeDtypeStruct((NY, NZ, own_rows, vocab), jnp.float32),
            jax.ShapeDtypeStruct((count, vocab), jnp.float32),
        ],
        scratch_shapes=[pltpu.VMEM((2 * count, vocab), jnp.float32)] * 2,
        cost_estimate=pl.CostEstimate(
            flops=2 * count * weight.size, bytes_accessed=2 * weight.size, transcendentals=0
        ),
        name="score",
    )(place, *blocks, weight, weight, columns, probs)


def gather_weight(weight):
    return lax.all_gather(weight.T, ("dp", "vocab"), axis=0, axis_index_groups=YC_GROUPS)


def layers(
    head_input,
    body_input,
    head_weight,
    gate_weight,
    up_weight,
    down_weight,
    tile_ids,
    tile_probs,
    tile_slot,
):
    shards = NY * NZ
    own_rows, width = head_input.shape
    slots, entries = tile_ids.shape
    vocab = head_weight.shape[0]
    count = shards * own_rows
    place = lax.axis_index("vocab")
    share = width // shards

    gate_full = gather_weight(gate_weight)
    up_full = gather_weight(up_weight)
    down_full = gather_weight(down_weight)

    quarter = width // NX
    packed = jnp.concatenate(
        [
            head_input.reshape(own_rows, 2, -1, 128).transpose(2, 1, 0, 3).reshape(-1, 128),
            (tile_ids // RADIX).astype(jnp.bfloat16).reshape(-1, 128),
            (tile_ids % RADIX).astype(jnp.bfloat16).reshape(-1, 128),
            tile_probs.reshape(-1, 128),
        ],
        axis=0,
    )
    size, whole = own_rows * width // 128, packed.shape[0]
    line = exchange(replicate(packed, NZ), Z_GROUPS)
    before = lax.ppermute(line, "vocab", Y_TURNS[1])
    after = lax.ppermute(line, "vocab", Y_TURNS[-1])
    far = [
        lax.ppermute(before[: NZ // 2], "vocab", Y_TURNS[1]),
        lax.ppermute(after[NZ // 2 :], "vocab", Y_TURNS[-1]),
    ]
    blocks = [line, before, after] + far

    body_tiles = as_tiles(body_input).reshape(NX, 1, -1, 128)
    body_tiles = jnp.broadcast_to(body_tiles, (NX, NZ) + body_tiles.shape[2:])
    body_tiles = exchange(
        body_tiles.reshape((NX * NZ,) + body_tiles.shape[2:]), XZ_GROUPS, ("dp", "vocab")
    )
    body_rows = from_tiles(body_tiles, own_rows)
    store = (
        jnp.concatenate([block[:, size:whole] for block in blocks])
        .reshape(shards, 3, slots, entries)
        .transpose(0, 2, 1, 3)
        .reshape(shards * slots, 3 * entries)
    )
    held = lax.broadcasted_iota(jnp.int32, (1, shards * slots), 1)
    line_slots = NZ * slots
    shift = jnp.zeros_like(held)
    for i, step in enumerate(LINES):
        shift = jnp.where(held // line_slots == i, step, shift)
    store_slot = (place // NZ + shift + NY) % NY * line_slots + held % line_slots
    chosen_slot = (tile_slot[:, None] == store_slot).astype(jnp.bfloat16)
    found = jnp.dot(chosen_slot, store, preferred_element_type=jnp.float32)
    row_ids = (found[:, :entries] * RADIX + found[:, entries : 2 * entries]).astype(jnp.int32)
    row_probs = found[:, 2 * entries :]
    tail_mass = 1.0 - jnp.sum(row_probs, axis=1, keepdims=True)
    logits, marks = score(
        (place // NZ).reshape(1), blocks, head_weight, row_ids - place * vocab, row_probs
    )
    logits = logits.reshape(count, vocab)
    picked = marks >= 0.0
    teacher = jnp.maximum(marks, 0.0)

    local_max = jnp.max(logits, axis=1, keepdims=True)
    rest = jnp.where(picked, -1e30, logits)
    local_rest_max = jnp.max(rest, axis=1, keepdims=True)
    local_top = jnp.sum(jnp.where(picked, jnp.exp(logits - local_max), 0.0), axis=1, keepdims=True)
    local_rest = jnp.sum(
        jnp.where(picked, 0.0, jnp.exp(rest - local_rest_max)), axis=1, keepdims=True
    )
    stats = jnp.concatenate([local_max, local_rest_max, local_top, local_rest], axis=1).T
    every = exchange(replicate(stats, shards))
    maxima, rest_maxima, tops, rests = jnp.split(every, 4, axis=1)
    row_max = jnp.max(maxima, axis=0)
    rest_max = jnp.max(rest_maxima, axis=0)
    top_sum = jnp.sum(tops * jnp.exp(maxima - row_max), axis=0)
    rest_sum = jnp.sum(rests * jnp.exp(rest_maxima - rest_max), axis=0)
    total = top_sum + rest_sum * jnp.exp(rest_max - row_max)
    row_max, rest_max, rest_sum, total, top_share = (
        value.reshape(count, 1) for value in (row_max, rest_max, rest_sum, total, top_sum / total)
    )
    student = jnp.exp(logits - row_max) / total
    spread = jnp.where(picked, 0.0, jnp.exp(rest - rest_max)) / rest_sum
    logit_grad = (
        LOSS_SCALE
        * (
            student * (1.0 - tail_mass)
            + jnp.where(picked, tail_mass * student - teacher, -tail_mass * top_share * spread)
        )
    ).astype(jnp.bfloat16)

    acts = wide(body_rows, gate_full, 0, 2)
    acts = wide(body_rows, up_full, 1, 2, acts)
    chip = lax.axis_index("dp") // CORES

    def turn_acts(step):
        block = lax.dynamic_index_in_dim(acts, (chip + step) % NX, 0, keepdims=False)
        return lax.ppermute(block, "dp", X_TURNS[step]) if step else block

    gathered = [turn_acts(step) for step in range(NX)]
    gate_act, up_act = sum(block.astype(jnp.float32) for block in gathered)

    arrived = exchange(head_blocks(logit_grad, head_weight), Y_GROUPS)
    over_y = add_blocks(arrived).astype(jnp.bfloat16)
    arrived = exchange(over_y, XZ_GROUPS, ("dp", "vocab"))
    head_own = jnp.sum(
        arrived.reshape((NX, NZ) + arrived.shape[1:]).astype(jnp.float32), axis=1
    ).astype(jnp.bfloat16)
    head_own = head_own.reshape(count, share)
    head_grad = (
        exchange(replicate(head_own, NZ), Z_GROUPS).transpose(1, 0, 2).reshape(count, quarter)
    )

    down_grad = add_blocks(exchange(wide(head_grad, down_full, 0, 1)[:, 0], X_GROUPS, "dp"))
    sigma = 1.0 / (1.0 + jnp.exp(-gate_act))
    gate_grad = (down_grad * up_act * sigma * (1.0 + gate_act * (1.0 - sigma))).astype(jnp.bfloat16)
    up_grad = (down_grad * gate_act * sigma).astype(jnp.bfloat16)
    both = exchange(replicate(jnp.stack([gate_grad, up_grad]), NX), X_GROUPS, "dp")
    pieces = branch_blocks(both, gate_full, up_full, head_own, (place % NZ).reshape(1))
    arrived = exchange(
        pieces.reshape((NX * NZ,) + pieces.shape[2:]), XZ_GROUPS, ("dp", "vocab")
    )
    grads = jnp.sum(arrived.reshape((NX, NZ) + arrived.shape[1:]).astype(jnp.float32), axis=1)
    return exchange(grads.astype(jnp.bfloat16), Y_GROUPS).reshape(count, share)


def solution(mesh):
    return jax.shard_map(
        layers,
        mesh=mesh,
        in_specs=(
            P(("dp", "vocab"), None),
            P(("dp", "vocab"), None),
            P("vocab", None),
            P("dp", "vocab"),
            P("dp", "vocab"),
            P("dp", "vocab"),
            P(("dp", "vocab"), None),
            P(("dp", "vocab"), None),
            P("dp"),
        ),
        out_specs=P("dp", "vocab"),
        check_vma=False,
    )
```

```python
import jax
import jax.numpy as jnp
from jax import lax
from jax.experimental import pallas as pl
from jax.experimental.pallas import tpu as pltpu
from jax.sharding import PartitionSpec as P


LOSS_SCALE = 1024
NX, NY, NZ, CORES = 4, 4, 8, 2
RADIX = 128

Y_GROUPS = [[y * NZ + z for y in range(NY)] for z in range(NZ)]
Z_GROUPS = [[y * NZ + z for z in range(NZ)] for y in range(NY)]
X_GROUPS = [[x * CORES + c for x in range(NX)] for c in range(CORES)]
YC_GROUPS = [
    [(x * CORES + c) * NY * NZ + y * NZ + z for y in range(NY) for c in range(CORES)]
    for x in range(NX)
    for z in range(NZ)
]

Y_TURNS = {
    step: [
        (y * NZ + z, (y + step) % NY * NZ + z) for y in range(NY) for z in range(NZ)
    ]
    for step in (1, -1, 2)
}
LINES = (0, -1, 1, 2)
X_TURNS = {
    step: [(x * CORES + c, (x + step) % NX * CORES + c) for x in range(NX) for c in range(CORES)]
    for step in range(1, NX)
}
XZ_GROUPS = [
    [(x * CORES + c) * NY * NZ + y * NZ + z for x in range(NX) for z in range(NZ)]
    for c in range(CORES)
    for y in range(NY)
]
Y_TURNS = {
    step: [
        (y * NZ + z, (y + step) % NY * NZ + z) for y in range(NY) for z in range(NZ)
    ]
    for step in (1, -1, 2)
}
LINES = (0, -1, 1, 2)
X_TURNS = {
    step: [(x * CORES + c, (x + step) % NX * CORES + c) for x in range(NX) for c in range(CORES)]
    for step in range(1, NX)
}
NT = (((1,), (1,)), ((), ()))
TN = (((0,), (0,)), ((), ()))


def exchange(blocks, groups=None, axis="vocab"):
    return lax.all_to_all(blocks, axis, 0, 0, axis_index_groups=groups)


def replicate(block, copies):
    return jnp.broadcast_to(block[None], (copies,) + block.shape)


def as_tiles(rows):
    count, width = rows.shape
    return rows.reshape(count, width // 128, 128).transpose(1, 0, 2).reshape(-1, 128)


def from_tiles(blocks, rows):
    shards, size, lanes = blocks.shape
    blocks = blocks.reshape(shards, size // rows, rows, lanes).transpose(0, 2, 1, 3)
    return blocks.reshape(shards * rows, size // rows * lanes)


def add_blocks(blocks):
    return jnp.sum(blocks.astype(jnp.float32), axis=0)


def wide_kernel(rows_ref, weight_ref, *refs):
    out_ref = refs[-1]
    half = weight_ref.shape[2]
    total = lax.dot_general(
        weight_ref[0], rows_ref[:, :half], NT, preferred_element_type=jnp.float32
    )
    total += lax.dot_general(
        weight_ref[1], rows_ref[:, half:], NT, preferred_element_type=jnp.float32
    )
    out_ref[0, 0] = total.astype(out_ref.dtype)


def wide(rows, weight, slot, entries, buffer=None):
    count = rows.shape[0]
    blocks, hidden, half = weight.shape
    parts = blocks // CORES
    in_specs = [
        pl.BlockSpec(rows.shape, lambda i: (0, 0)),
        pl.BlockSpec((CORES, hidden, half), lambda i: (i, 0, 0)),
    ]
    args = (rows, weight)
    if buffer is not None:
        in_specs.append(pl.BlockSpec(memory_space=pl.ANY))
        args += (buffer,)
    return pl.pallas_call(
        wide_kernel,
        grid=(parts,),
        in_specs=in_specs,
        out_specs=pl.BlockSpec((1, 1, hidden, count), lambda i: (i, slot, 0, 0)),
        out_shape=jax.ShapeDtypeStruct((parts, entries, hidden, count), jnp.bfloat16),
        input_output_aliases={} if buffer is None else {2: 0},
        cost_estimate=pl.CostEstimate(
            flops=2 * count * blocks * hidden * half,
            bytes_accessed=2 * (weight.size + rows.size),
            transcendentals=0,
        ),
        name="wide",
    )(*args)


def branch_kernel(place_ref, act_ref, gate_weight_ref, up_weight_ref, extra_ref, out_ref):
    parts, _, hidden, count = act_ref.shape
    total = 0.0
    for k, weight in enumerate((gate_weight_ref, up_weight_ref)):
        total += lax.dot_general(
            act_ref[:, k].reshape(parts * hidden, count),
            weight[:, 0].reshape(parts * hidden, weight.shape[3]),
            TN,
            preferred_element_type=jnp.float32,
        )
    total += jnp.where(pl.program_id(0) == place_ref[0], extra_ref[...].astype(jnp.float32), 0.0)
    parts, _, rows, share = out_ref.shape
    out_ref[:, 0] = total.reshape(parts, rows, share).astype(out_ref.dtype)


def branch_blocks(acts, gate_weight, up_weight, extra, place):
    parts, _, hidden, count = acts.shape
    half = gate_weight.shape[2]
    share = CORES * half // NZ
    per = half // share
    gate_weight = gate_weight.reshape(parts, CORES, hidden, half)
    up_weight = up_weight.reshape(parts, CORES, hidden, half)
    weight_spec = pl.BlockSpec((parts, 1, hidden, share), lambda i: (0, i // per, 0, i % per))
    return pl.pallas_call(
        branch_kernel,
        grid=(NZ,),
        in_specs=[
            pl.BlockSpec(memory_space=pltpu.SMEM),
            pl.BlockSpec(acts.shape, lambda i: (0, 0, 0, 0)),
            weight_spec,
            weight_spec,
            pl.BlockSpec(extra.shape, lambda i: (0, 0)),
        ],
        out_specs=pl.BlockSpec((NX, 1, count // NX, share), lambda i: (0, i, 0, 0)),
        out_shape=jax.ShapeDtypeStruct((NX, NZ, count // NX, share), jnp.bfloat16),
        cost_estimate=pl.CostEstimate(
            flops=4 * count * gate_weight.size,
            bytes_accessed=4 * gate_weight.size,
            transcendentals=0,
        ),
        name="branch",
    )(place, acts, gate_weight, up_weight, extra)


def head_kernel(grad_ref, weight_ref, out_ref):
    quarters, steps, rows, share = out_ref.shape
    for i in range(steps):
        part = jnp.dot(
            grad_ref[...],
            weight_ref[:, i * share : (i + 1) * share],
            preferred_element_type=jnp.float32,
        )
        out_ref[:, i] = part.reshape(quarters, rows, share).astype(out_ref.dtype)


def head_blocks(grad, weight):
    count, vocab = grad.shape
    width = weight.shape[1]
    parts = NX * NZ
    share = width // parts
    step = 4
    return pl.pallas_call(
        head_kernel,
        grid=(parts // step,),
        in_specs=[
            pl.BlockSpec(grad.shape, lambda i: (0, 0)),
            pl.BlockSpec((vocab, step * share), lambda i: (0, i)),
        ],
        out_specs=pl.BlockSpec((NY, step, count // NY, share), lambda i: (0, i, 0, 0)),
        out_shape=jax.ShapeDtypeStruct((NY, parts, count // NY, share), jnp.bfloat16),
        cost_estimate=pl.CostEstimate(
            flops=2 * count * weight.size,
            bytes_accessed=2 * weight.size,
            transcendentals=0,
        ),
        name="head",
    )(grad, weight)


def marks_kernel(columns_ref, probs_ref, out_ref):
    entries = columns_ref.shape[1]
    places = lax.broadcasted_iota(jnp.int32, out_ref.shape, 1)
    columns = columns_ref[...]
    probs = probs_ref[...]
    marks = jnp.full(out_ref.shape, -1.0, jnp.float32)
    for k in range(entries):
        marks = jnp.where(places == columns[:, k : k + 1], probs[:, k : k + 1], marks)
    out_ref[...] = marks


def make_marks(columns, probs, vocab):
    count, entries = columns.shape
    step = 16
    spec = pl.BlockSpec((step, entries), lambda i: (i, 0))
    return pl.pallas_call(
        marks_kernel,
        grid=(count // step,),
        in_specs=[spec, spec],
        out_specs=pl.BlockSpec((step, vocab), lambda i: (i, 0)),
        out_shape=jax.ShapeDtypeStruct((count, vocab), jnp.float32),
        cost_estimate=pl.CostEstimate(
            flops=2 * count * entries * vocab, bytes_accessed=4 * count * vocab, transcendentals=0
        ),
        name="marks",
    )(columns, probs)


def score_kernel(place_ref, *refs):
    *block_refs, low_ref, high_ref, marks_ref = refs[:-4]
    logits_ref, stats_ref, low_sum, high_sum = refs[-4:]
    step = pl.program_id(0)
    shards = NY * NZ
    count, vocab = logits_ref.shape
    both = 2 * count // shards

    def tile(block_ref, i):
        held, _, lanes = block_ref.shape
        return block_ref[:, i * both : (i + 1) * both].reshape(held * both, lanes)

    rows = jnp.concatenate(
        [
            jnp.concatenate([tile(block_ref, i) for block_ref in block_refs], axis=0)
            for i in range(block_refs[0].shape[1] // both)
        ],
        axis=1,
    )
    for weight_ref, total in ((low_ref, low_sum), (high_ref, high_sum)):
        part = lax.dot_general(rows, weight_ref[...], NT, preferred_element_type=jnp.float32)
        total[...] = jnp.where(step == 0, 0.0, total[...]) + part

    @pl.when(step == pl.num_programs(0) - 1)
    def _():
        low = low_sum[...].reshape(shards, both, vocab)
        high = high_sum[...].reshape(shards, both, vocab)
        sums = (low[:, : both // 2] + high[:, both // 2 :]).reshape(count, vocab)
        size = count // NY
        for i, line in enumerate(LINES):
            start = lax.rem(place_ref[0] + line + NY, NY) * size
            logits_ref[pl.ds(pl.multiple_of(start, size), size)] = sums[i * size : (i + 1) * size]
        logits = logits_ref[...]
        picked = marks_ref[...] >= 0.0
        most = jnp.max(logits, axis=1, keepdims=True)
        rest = jnp.where(picked, -1e30, logits)
        rest_most = jnp.max(rest, axis=1, keepdims=True)
        top = jnp.sum(jnp.where(picked, jnp.exp(logits - most), 0.0), axis=1, keepdims=True)
        others = jnp.sum(jnp.where(picked, 0.0, jnp.exp(rest - rest_most)), axis=1, keepdims=True)
        lane = lax.broadcasted_iota(jnp.int32, (count, 128), 1)
        table = jnp.where(lane == 2, top, others)
        table = jnp.where(lane == 1, rest_most, table)
        table = jnp.where(lane == 0, most, table)
        stats_ref[...] = table.T[:4]


def score(place, blocks, weight, marks):
    count, vocab = marks.shape
    width = weight.shape[1]
    own_rows = count // (NY * NZ)
    steps = 8
    chunk = width // 2 // steps
    size = chunk // 128 * 2 * own_rows
    return pl.pallas_call(
        score_kernel,
        grid=(steps,),
        in_specs=[pl.BlockSpec(memory_space=pltpu.SMEM)]
        + [pl.BlockSpec((block.shape[0], size, 128), lambda i: (0, i, 0)) for block in blocks]
        + [
            pl.BlockSpec((vocab, chunk), lambda i: (0, i)),
            pl.BlockSpec((vocab, chunk), lambda i: (0, i + steps)),
            pl.BlockSpec((count, vocab), lambda i: (0, 0)),
        ],
        out_specs=[
            pl.BlockSpec((count, vocab), lambda i: (0, 0)),
            pl.BlockSpec((4, count), lambda i: (0, 0)),
        ],
        out_shape=[
            jax.ShapeDtypeStruct((count, vocab), jnp.float32),
            jax.ShapeDtypeStruct((4, count), jnp.float32),
        ],
        scratch_shapes=[pltpu.VMEM((2 * count, vocab), jnp.float32)] * 2,
        cost_estimate=pl.CostEstimate(
            flops=2 * count * weight.size, bytes_accessed=2 * weight.size, transcendentals=0
        ),
        name="score",
    )(place, *blocks, weight, weight, marks)


def gather_weight(weight):
    return lax.all_gather(weight.T, ("dp", "vocab"), axis=0, axis_index_groups=YC_GROUPS)


def layers(
    head_input,
    body_input,
    head_weight,
    gate_weight,
    up_weight,
    down_weight,
    tile_ids,
    tile_probs,
    tile_slot,
):
    shards = NY * NZ
    own_rows, width = head_input.shape
    slots, entries = tile_ids.shape
    vocab = head_weight.shape[0]
    count = shards * own_rows
    place = lax.axis_index("vocab")
    share = width // shards

    gate_full = gather_weight(gate_weight)
    up_full = gather_weight(up_weight)
    down_full = gather_weight(down_weight)

    quarter = width // NX
    packed = jnp.concatenate(
        [
            head_input.reshape(own_rows, 2, -1, 128).transpose(2, 1, 0, 3).reshape(-1, 128),
            (tile_ids // RADIX).astype(jnp.bfloat16).reshape(-1, 128),
            (tile_ids % RADIX).astype(jnp.bfloat16).reshape(-1, 128),
            tile_probs.reshape(-1, 128),
        ],
        axis=0,
    )
    size, whole = own_rows * width // 128, packed.shape[0]
    line = exchange(replicate(packed, NZ), Z_GROUPS)
    before = lax.ppermute(line, "vocab", Y_TURNS[1])
    after = lax.ppermute(line, "vocab", Y_TURNS[-1])
    tiles = line[:, size:whole]
    tiles = [tiles] + [lax.ppermute(tiles, "vocab", Y_TURNS[step]) for step in (1, -1, 2)]
    far = [
        lax.ppermute(before[: NZ // 2], "vocab", Y_TURNS[1]),
        lax.ppermute(after[NZ // 2 :], "vocab", Y_TURNS[-1]),
    ]
    blocks = [line, before, after] + far

    body_tiles = as_tiles(body_input).reshape(NX, 1, -1, 128)
    body_tiles = jnp.broadcast_to(body_tiles, (NX, NZ) + body_tiles.shape[2:])
    body_tiles = exchange(
        body_tiles.reshape((NX * NZ,) + body_tiles.shape[2:]), XZ_GROUPS, ("dp", "vocab")
    )
    body_rows = from_tiles(body_tiles, own_rows)
    store = (
        jnp.concatenate(tiles)
        .reshape(shards, 3, slots, entries)
        .transpose(0, 2, 1, 3)
        .reshape(shards * slots, 3 * entries)
    )
    held = lax.broadcasted_iota(jnp.int32, (1, shards * slots), 1)
    line_slots = NZ * slots
    shift = jnp.zeros_like(held)
    for i, step in enumerate(LINES):
        shift = jnp.where(held // line_slots == i, step, shift)
    store_slot = (place // NZ + shift + NY) % NY * line_slots + held % line_slots
    chosen_slot = (tile_slot[:, None] == store_slot).astype(jnp.bfloat16)
    found = jnp.dot(chosen_slot, store, preferred_element_type=jnp.float32)
    row_ids = (found[:, :entries] * RADIX + found[:, entries : 2 * entries]).astype(jnp.int32)
    row_probs = found[:, 2 * entries :]
    tail_mass = 1.0 - jnp.sum(row_probs, axis=1, keepdims=True)
    marks = make_marks(row_ids - place * vocab, row_probs, vocab)
    logits, stats = score((place // NZ).reshape(1), blocks, head_weight, marks)
    picked = marks >= 0.0
    teacher = jnp.maximum(marks, 0.0)
    every = exchange(replicate(stats, shards))
    maxima, rest_maxima, tops, rests = jnp.split(every, 4, axis=1)
    row_max = jnp.max(maxima, axis=0)
    rest_max = jnp.max(rest_maxima, axis=0)
    top_sum = jnp.sum(tops * jnp.exp(maxima - row_max), axis=0)
    rest_sum = jnp.sum(rests * jnp.exp(rest_maxima - rest_max), axis=0)
    total = top_sum + rest_sum * jnp.exp(rest_max - row_max)
    row_max, rest_max, rest_sum, total, top_share = (
        value.reshape(count, 1) for value in (row_max, rest_max, rest_sum, total, top_sum / total)
    )
    student = jnp.exp(logits - row_max) / total
    rest = jnp.where(picked, -1e30, logits)
    spread = jnp.where(picked, 0.0, jnp.exp(rest - rest_max)) / rest_sum
    logit_grad = (
        LOSS_SCALE
        * (
            student * (1.0 - tail_mass)
            + jnp.where(picked, tail_mass * student - teacher, -tail_mass * top_share * spread)
        )
    ).astype(jnp.bfloat16)

    acts = wide(body_rows, gate_full, 0, 2)
    acts = wide(body_rows, up_full, 1, 2, acts)
    chip = lax.axis_index("dp") // CORES

    def turn_acts(step):
        block = lax.dynamic_index_in_dim(acts, (chip + step) % NX, 0, keepdims=False)
        return lax.ppermute(block, "dp", X_TURNS[step]) if step else block

    gathered = [turn_acts(step) for step in range(NX)]
    gate_act, up_act = sum(block.astype(jnp.float32) for block in gathered)

    arrived = exchange(head_blocks(logit_grad, head_weight), Y_GROUPS)
    over_y = add_blocks(arrived).astype(jnp.bfloat16)
    arrived = exchange(over_y, XZ_GROUPS, ("dp", "vocab"))
    head_own = jnp.sum(
        arrived.reshape((NX, NZ) + arrived.shape[1:]).astype(jnp.float32), axis=1
    ).astype(jnp.bfloat16)
    head_own = head_own.reshape(count, share)
    head_grad = (
        exchange(replicate(head_own, NZ), Z_GROUPS).transpose(1, 0, 2).reshape(count, quarter)
    )

    down_grad = add_blocks(exchange(wide(head_grad, down_full, 0, 1)[:, 0], X_GROUPS, "dp"))
    sigma = 1.0 / (1.0 + jnp.exp(-gate_act))
    gate_grad = (down_grad * up_act * sigma * (1.0 + gate_act * (1.0 - sigma))).astype(jnp.bfloat16)
    up_grad = (down_grad * gate_act * sigma).astype(jnp.bfloat16)
    both = exchange(replicate(jnp.stack([gate_grad, up_grad]), NX), X_GROUPS, "dp")
    pieces = branch_blocks(both, gate_full, up_full, head_own, (place % NZ).reshape(1))
    arrived = exchange(
        pieces.reshape((NX * NZ,) + pieces.shape[2:]), XZ_GROUPS, ("dp", "vocab")
    )
    grads = jnp.sum(arrived.reshape((NX, NZ) + arrived.shape[1:]).astype(jnp.float32), axis=1)
    return exchange(grads.astype(jnp.bfloat16), Y_GROUPS).reshape(count, share)


def solution(mesh):
    return jax.shard_map(
        layers,
        mesh=mesh,
        in_specs=(
            P(("dp", "vocab"), None),
            P(("dp", "vocab"), None),
            P("vocab", None),
            P("dp", "vocab"),
            P("dp", "vocab"),
            P("dp", "vocab"),
            P(("dp", "vocab"), None),
            P(("dp", "vocab"), None),
            P("dp"),
        ),
        out_specs=P("dp", "vocab"),
        check_vma=False,
    )
```
